32 devices in a mesh: dp: 8 (over y, x, core), seq: 4 (over z).
Axes of the slice: x: 2, y: 2, z: 4, core: 2. Of those that a mesh axis runs over, the one named last changes fastest.
Arguments:
- coarse: bfloat16 [8, 256, 1536], P('dp', 'seq'), may hold values from -6 to 6
- skip_feats: bfloat16 [8, 512, 1536], P('dp', 'seq'), may hold values from -6 to 6
- conv_taps: float32 [3, 1536], replicated, may hold values from -3 to 3
- norm_gain: float32 [1536], replicated, may hold values from 0.5 to 1.5
- head_weight: bfloat16 [1536, 4096], P(None, 'dp'), may hold values from -0.15625 to 0.15625
- adapter_down: bfloat16 [1536, 16], replicated, may hold values from -0.15625 to 0.15625
- adapter_up: bfloat16 [16, 4096], replicated, may hold values from -1.5 to 1.5
- head_bias: float32 [4096], replicated, may hold values from -3 to 3
- exon_bins: int32 [8, 16, 32], P('dp', 'seq'), may hold values from 0 to 511, as said below
- exon_count: int32 [8, 16], P('dp', 'seq'), may hold values from 1 to 32, as said below
- targets: int32 [8, 16, 4096], P('dp'), may hold values from 0 to 543
Outputs:
- coverage: float32 [8, 16, 4096], P('dp', 'seq')
- loss: float32 [], replicated
- grad_down: float32 [1536, 16], replicated
- grad_up: float32 [16, 4096], replicated
- grad_bias: float32 [4096], replicated
The draws below stay inside these ranges and needn't reach their ends.
Inputs may be any that keep to these rules, and one draw needn't show every extreme that they name: `exon_count`: every window has a gene whose list has all 32 slots live; slots at or past a gene's count hold bins that are to be ignored. `exon_bins`: each gene's bins lie within one span of consecutive bins of its window and are listed in ascending order.
All inputs are finite; a program needn't handle non-finite values.
Results may differ from the reference program's by a relative error of at most 0.00072.
Values may be sent and summed in bfloat16 or wider, within the bound.
A program may use at most 64 MiB of HBM per device.

```python
import jax
import jax.numpy as jnp
from jax import lax

C = 1536
TRACKS = 4096
RANK = 16
BINS_DEV = 128
MAXEX = 32
BINS = 512
WINDOWS = 8
GENES = 16


def draw_exon_count(key, part):
    first, second = jax.random.split(jax.random.fold_in(key, 17))
    counts = jax.random.randint(first, (WINDOWS, GENES), 1, MAXEX + 1)
    chosen = jax.random.randint(second, (WINDOWS, 1), 0, GENES)
    return jnp.where(jnp.arange(GENES)[None, :] == chosen, MAXEX, counts).astype(jnp.int32)


def draw_exon_bins(key, part):
    keys = jax.random.split(jax.random.fold_in(key, 29), 4)
    unit = max(BINS_DEV // 4, 1)
    levels = jax.random.randint(keys[0], (WINDOWS, GENES), 0, 5).astype(jnp.int32)
    basic = jnp.left_shift(jnp.full((WINDOWS, GENES), unit, jnp.int32), levels)
    extra = jax.random.randint(keys[1], (WINDOWS, GENES), 0, 1 << 20).astype(jnp.int32) % basic
    length = jnp.minimum(basic + extra, BINS).astype(jnp.int32)
    room = BINS - length + 1
    start = (jax.random.randint(keys[2], (WINDOWS, GENES), 0, 1 << 20).astype(jnp.int32) % room).astype(jnp.int32)
    gene_index = jnp.arange(GENES, dtype=jnp.int32)[None, :]
    start = jnp.where(gene_index == 0, 0, start)
    start = jnp.where(gene_index == GENES - 1, BINS - length, start).astype(jnp.int32)
    offsets = jax.random.randint(keys[3], (WINDOWS, GENES, MAXEX), 0, 1 << 20).astype(jnp.int32) % length[:, :, None]
    slot_index = jnp.arange(MAXEX, dtype=jnp.int32)[None, None, :]
    offsets = jnp.where(slot_index == 0, 0, offsets)
    offsets = jnp.where(slot_index == MAXEX - 1, length[:, :, None] - 1, offsets)
    offsets = jnp.sort(offsets, axis=-1)
    return (start[:, :, None] + offsets).astype(jnp.int32)


def draw_targets(key, part):
    base = jax.random.randint(jax.random.fold_in(key, 41), (WINDOWS, GENES, TRACKS), 0, MAXEX).astype(jnp.int32)
    track_index = jnp.arange(TRACKS, dtype=jnp.int32)
    owner = track_index * WINDOWS // TRACKS
    window_index = jnp.arange(WINDOWS, dtype=jnp.int32)
    heavy = owner[None, None, :] == window_index[:, None, None]
    values = base + jnp.where(heavy, 16 * MAXEX, 0).astype(jnp.int32)
    gene_index = jnp.arange(GENES, dtype=jnp.int32)
    corner = (window_index[:, None, None] == 0) & (gene_index[None, :, None] == 0)
    values = jnp.where(corner & (track_index[None, None, :] == 0), 17 * MAXEX - 1, values)
    values = jnp.where(corner & (track_index[None, None, :] == TRACKS - 1), 0, values)
    return values.astype(jnp.int32)


def block_levels(own_key, dims, cuts, smallest, high):
    level, own = 1.0, jax.random.fold_in(own_key, 6)
    for dim, shards_of in cuts:
        draws = jnp.exp(jax.random.uniform(jax.random.fold_in(own, dim), (shards_of,), jnp.float32, smallest / len(cuts), high / len(cuts)))
        level = level * jnp.repeat(draws, dims[dim] // shards_of).reshape([-1 if axis == dim else 1 for axis in range(len(dims))])
    return level


def normal_values(stream_key, dims, width, most, shards=(), held_as=jnp.bfloat16):
    array = width * jax.random.normal(stream_key, dims, jnp.float32)
    if shards:
        array = array * block_levels(stream_key, dims, shards, -0.22, 0.18)
    return jnp.clip(array, -most, most).astype(held_as)


def setup_inputs(seed: int = 0) -> dict:
    arg_keys = jax.random.split(jax.random.key(seed), 12)
    coarse = normal_values(arg_keys[0], (WINDOWS, BINS // 2, C), 1.0, 6.0, ((0, 8), (1, 4)))
    skip_feats = normal_values(arg_keys[1], (WINDOWS, BINS, C), 1.0, 6.0, ((0, 8), (1, 4)))
    conv_taps = normal_values(arg_keys[2], (3, C), 0.6, 3.0, (), jnp.float32)
    norm_gain = jnp.clip(1.0 + 0.1 * jax.random.normal(arg_keys[3], (C,), jnp.float32), 0.5, 1.5)
    head_weight = normal_values(arg_keys[4], (C, TRACKS), C ** -0.5, 0.15625, ((1, 8),))
    adapter_down = normal_values(arg_keys[5], (C, RANK), C ** -0.5, 0.15625)
    adapter_up = normal_values(arg_keys[6], (RANK, TRACKS), RANK ** -0.5, 1.5)
    head_bias = normal_values(arg_keys[7], (TRACKS,), 0.5, 3.0, (), jnp.float32)
    exon_bins = draw_exon_bins(jax.random.fold_in(arg_keys[11], 71), 0)
    exon_count = draw_exon_count(jax.random.fold_in(arg_keys[11], 71), 0)
    targets = draw_targets(jax.random.fold_in(arg_keys[11], 71), 0)
    return dict(coarse=coarse, skip_feats=skip_feats, conv_taps=conv_taps, norm_gain=norm_gain, head_weight=head_weight, adapter_down=adapter_down, adapter_up=adapter_up, head_bias=head_bias, exon_bins=exon_bins, exon_count=exon_count, targets=targets)


def gelu_norm(mixed, norm_gain):
    normed = mixed * lax.rsqrt(lax.optimization_barrier(jnp.mean(mixed * mixed, axis=-1, keepdims=True)) + 1e-06) * norm_gain
    return jax.nn.gelu(normed).astype(jnp.bfloat16)

def reference(coarse, skip_feats, conv_taps, norm_gain, head_weight, adapter_down, adapter_up, head_bias, exon_bins, exon_count, targets):
    scale = 1.0 / (WINDOWS * GENES)

    def one_window(carry, items):
        low_rows, skip_rows, bins, counts, wanted = items
        merged = (jnp.repeat(low_rows, 2, axis=0).astype(jnp.float32) + skip_rows.astype(jnp.float32)).astype(jnp.bfloat16)
        padded = jnp.pad(merged, ((1, 1), (0, 0))).astype(jnp.float32)
        mixed = conv_taps[0] * padded[:-2] + conv_taps[1] * padded[1:-1] + conv_taps[2] * padded[2:]
        hidden = gelu_norm(mixed, norm_gain)
        reduced = jnp.dot(hidden, adapter_down, preferred_element_type=jnp.float32).astype(jnp.bfloat16)
        head_out = jnp.dot(hidden, head_weight, preferred_element_type=jnp.float32) + jnp.dot(reduced, adapter_up, preferred_element_type=jnp.float32) + head_bias
        predicted = jax.nn.softplus(head_out)
        live = (jnp.arange(MAXEX)[None, :] < counts[:, None]).astype(jnp.float32)
        picked = predicted[bins]
        coverage = lax.optimization_barrier(jnp.sum(picked * live[:, :, None], axis=1))
        wanted_f = wanted.astype(jnp.float32)
        loss = scale * jnp.sum(coverage - wanted_f * jnp.log1p(coverage))
        slopes = scale * (1.0 - wanted_f / (1.0 + coverage))
        contrib = (live[:, :, None] * slopes[:, None, :]).reshape(-1, slopes.shape[1])
        spread = jnp.zeros_like(predicted).at[bins.reshape(-1)].add(contrib)
        grad_out = spread * jax.nn.sigmoid(head_out)
        grad_half = grad_out.astype(jnp.bfloat16)
        grad_up = jnp.dot(reduced.T, grad_half, preferred_element_type=jnp.float32)
        back = jnp.dot(grad_half, adapter_up.T, preferred_element_type=jnp.float32).astype(jnp.bfloat16)
        grad_down = jnp.dot(hidden.T, back, preferred_element_type=jnp.float32)
        grad_bias = lax.optimization_barrier(jnp.sum(grad_out, axis=0))
        total_down, total_up, total_bias, total_loss = carry
        return ((total_down + grad_down, total_up + grad_up, total_bias + grad_bias, total_loss + loss), coverage)
    start = (jnp.zeros((C, RANK), jnp.float32), jnp.zeros((RANK, TRACKS), jnp.float32), jnp.zeros((TRACKS,), jnp.float32), jnp.zeros((), jnp.float32))
    totals, coverage = lax.scan(one_window, start, (coarse, skip_feats, exon_bins, exon_count, targets))
    grad_down, grad_up, grad_bias, loss = totals
    return (coverage, loss, grad_down, grad_up, grad_bias)
```

```python
import functools

import jax
import jax.numpy as jnp
from jax import lax
from jax.experimental import pallas as pl
from jax.experimental.pallas import tpu as pltpu
from jax.sharding import PartitionSpec as P

MESH = pl.DeviceIdType.MESH
F32 = jnp.float32
BF16 = jnp.bfloat16
PARTS = 4


def mm(a, b):
    return jnp.dot(a, b, preferred_element_type=F32)


def mm_nt(a, b):
    return lax.dot_general(a, b, (((1,), (1,)), ((), ())), preferred_element_type=F32)


def mm_tn(a, b):
    return lax.dot_general(a, b, (((0,), (0,)), ((), ())), preferred_element_type=F32)


def kernel(
    n,
    m,
    scale,
    coarse_h,
    skip_h,
    taps_h,
    gain_h,
    weight,
    down_h,
    up_h,
    bias_h,
    bins_h,
    count_h,
    targets,
    cov_out,
    loss_out,
    down_out,
    up_out,
    bias_out,
    coarse,
    skip,
    taps,
    gain,
    down,
    up,
    bias,
    bins,
    count,
    w_vm,
    hid,
    aux,
    halo,
    edge,
    binbuf,
    tgt,
    sig,
    covp,
    covr,
    covt,
    slp,
    covin,
    bkp,
    bkr,
    bk,
    acc,
    ups,
    dns,
    fin,
    dnf,
    sem_loc,
    halo_s,
    halo_r,
    bin_s,
    bin_r,
    relay_s,
    relay_r,
    hid_s,
    fwd_s,
    hid_r,
    aux_s,
    aux_r,
    tgt_s,
    tgt_r,
    cov_s,
    cov_r,
    slp_s,
    slp_r,
    b1_s,
    b1_r,
    b2_s,
    b2_r,
    co_s,
    co_r,
    us_s,
    us_r,
    ds_s,
    ds_r,
    fu_s,
    fu_r,
    fd_s,
    fd_r,
):
    d = lax.axis_index("dp")
    s = lax.axis_index("seq")
    nc = n // 2
    relay = nc == 4
    chip = d // 2
    core = d % 2
    sib = chip * 2 + (1 - core)
    rows, chans = skip.shape[1], skip.shape[2]
    cols = weight.shape[1]
    owned = bins.shape[1]
    slots = bins.shape[2]
    rank = up.shape[0]
    genes = owned * m
    wide = chans // PARTS

    def pair_of(q):
        found, bit = 0, 1
        while bit < nc:
            found = found + bit * (((chip // bit) % 2 + (q // bit) % 2) % 2)
            bit *= 2
        return found

    def send(src, dst, ss, rs, dd, jj):
        return pltpu.make_async_remote_copy(
            src_ref=src,
            dst_ref=dst,
            send_sem=ss,
            recv_sem=rs,
            device_id=(dd, jj),
            device_id_type=MESH,
        )

    def dp_peer(k):
        return (d + k) % n

    def seq_peer(k):
        return (s + k) % m

    def column(k):
        return pl.ds(pl.multiple_of(k * cols, 128), cols)

    loads = []
    for src, dst in (
        (skip_h, skip),
        (coarse_h, coarse),
        (bins_h, bins),
        (count_h, count),
        (taps_h, taps),
        (gain_h, gain),
        (down_h, down),
        (up_h.at[:, column(d)], up),
        (bias_h.at[:, column(d)], bias),
        (weight, w_vm),
    ):
        c = pltpu.make_async_copy(src, dst, sem_loc.at[2 + len(loads)])
        c.start()
        loads.append(c)
    barrier = pltpu.get_barrier_semaphore()
    for k in range(1, n):
        pl.semaphore_signal(barrier, inc=1, device_id=(dp_peer(k), s), device_id_type=MESH)
    for k in range(1, m):
        pl.semaphore_signal(barrier, inc=1, device_id=(d, seq_peer(k)), device_id_type=MESH)

    for c in loads[:4]:
        c.wait()
    rr = lax.broadcasted_iota(jnp.int32, (rows, rows // 2), 0)
    cc = lax.broadcasted_iota(jnp.int32, (rows, rows // 2), 1)
    spread2 = jnp.where(rr // 2 == cc, 1.0, 0.0).astype(BF16)
    merged = (mm(spread2, coarse[0]) + skip[0].astype(F32)).astype(BF16).astype(F32)
    edge[0] = merged[0:1]
    edge[1] = merged[rows - 1 : rows]

    cnt = jnp.broadcast_to(count[...].astype(F32), (owned, owned))
    er = lax.broadcasted_iota(jnp.int32, (owned, owned), 0)
    ec = lax.broadcasted_iota(jnp.int32, (owned, owned), 1)
    cnt = jnp.sum(jnp.where(er == ec, cnt, 0.0), axis=1, keepdims=True)
    slot = lax.broadcasted_iota(jnp.int32, (owned, slots), 1).astype(F32)
    binbuf[s] = jnp.full((8, 128), -1, jnp.int32)
    binbuf[s, 0:owned, 0:slots] = jnp.where(slot < cnt, bins[0], -1)

    pl.semaphore_wait(barrier, n + m - 2)

    to_next = send(edge.at[1], halo.at[0], halo_s.at[0], halo_r.at[0], d, (s + 1) % m)
    to_prev = send(edge.at[0], halo.at[1], halo_s.at[1], halo_r.at[1], d, (s + m - 1) % m)

    @pl.when(s < m - 1)
    def _():
        to_next.start()

    @pl.when(s > 0)
    def _():
        to_prev.start()

    @pl.when(s == 0)
    def _():
        halo[0] = jnp.zeros((1, chans), F32)

    @pl.when(s == m - 1)
    def _():
        halo[1] = jnp.zeros((1, chans), F32)

    bin_copies = []
    for k in range(1, m):
        c = send(binbuf.at[s], binbuf.at[s], bin_s.at[k], bin_r.at[s], d, seq_peer(k))
        c.start()
        bin_copies.append(c)

    tile = 8 * (s * owned // 8)

    def tgt_src(k):
        return targets.at[0, pl.ds(pl.multiple_of(tile, 8), 8), column(k)]

    own_tgt = pltpu.make_async_copy(tgt_src(d), tgt.at[d], sem_loc.at[1])
    own_tgt.start()
    tgt_copies = []
    for k in range(1, n):
        c = send(tgt_src(dp_peer(k)), tgt.at[d], tgt_s.at[k], tgt_r.at[d], dp_peer(k), s)
        c.start()
        tgt_copies.append(c)

    @pl.when(s > 0)
    def _():
        to_next.wait_recv()

    @pl.when(s < m - 1)
    def _():
        to_prev.wait_recv()

    for c in loads[4:7]:
        c.wait()
    row = lax.broadcasted_iota(jnp.int32, (rows, chans), 0)
    before = jnp.where(row == 0, halo[0], pltpu.roll(merged, 1, 0))
    after = jnp.where(row == rows - 1, halo[1], pltpu.roll(merged, rows - 1, 0))
    mixed = taps[0:1] * before + taps[1:2] * merged + taps[2:3] * after
    normed = mixed * lax.rsqrt(jnp.mean(mixed * mixed, axis=-1, keepdims=True) + 1e-06) * gain[...].reshape(1, chans)
    hidden = jax.nn.gelu(normed).astype(BF16)
    hid[d] = hidden

    hid_copies = []
    for k in range(1, 3 if relay else nc):
        c = send(hid.at[d], hid.at[d], hid_s.at[k], hid_r.at[d], pair_of(k) * 2 + core, s)
        c.start()
        hid_copies.append(c)
    c = send(hid.at[d], hid.at[d], hid_s.at[0], hid_r.at[d], sib, s)
    c.start()
    hid_copies.append(c)

    aux[d, 0:rank] = mm_nt(down[...], hidden).astype(BF16)

    for k in range(1, m):
        j = seq_peer(k)
        send(binbuf.at[j], binbuf.at[j], bin_s.at[k], bin_r.at[j], d, j).wait_recv()
    listed = jnp.concatenate([binbuf[j][0:owned] for j in range(m)], axis=0)
    here = s * rows + lax.broadcasted_iota(jnp.int32, (genes, rows), 1)
    member = jnp.zeros((genes, rows), F32)
    for j in range(slots):
        member += jnp.where(listed[:, j : j + 1] == here, 1.0, 0.0)
    aux[d, rank : rank + genes] = member.astype(BF16)

    aux_copies = []
    for k in range(1, n):
        c = send(aux.at[d], aux.at[d], aux_s.at[k], aux_r.at[d], dp_peer(k), s)
        c.start()
        aux_copies.append(c)

    own_tgt.wait()
    for k in range(1, n):
        j = dp_peer(k)
        send(tgt.at[j], tgt.at[j], tgt_s.at[k], tgt_r.at[j], j, s).wait_recv()
    for c in loads[7:]:
        c.wait()
    acc[...] = jnp.zeros(acc.shape, F32)

    def window(p, u):
        return 2 * p + (core if u == 0 else 1 - core)

    def forward(w):
        return send(hid.at[w], hid.at[w], fwd_s.at[w], hid_r.at[w], sib, s)

    half = rows // 2

    def relay_copy(k):
        w = 2 * pair_of(k) + core
        part = hid.at[w, (k - 1) * half : k * half]
        there = 2 * pair_of(3 - k) + core
        return send(part, part, relay_s.at[k - 1], relay_r.at[k - 1], there, s)

    def relay_wait(k):
        part = hid.at[2 * pair_of(3) + core, (k - 1) * half : k * half]
        send(part, part, relay_s.at[k - 1], relay_r.at[k - 1], sib, s).wait_recv()

    def cov_copy(p, j):
        return send(covp.at[p, j], covr.at[p, s], cov_s.at[p, j], cov_r.at[p, s], d, j)

    def slp_copy(p, k):
        return send(slp.at[p, s], slp.at[p, s], slp_s.at[p, k], slp_r.at[p, s], d, seq_peer(k))

    def out_copy(p, w):
        return send(covt.at[p], covin.at[d], co_s.at[w], co_r.at[d], w, s)

    def back_copy(w):
        return send(bkp.at[w], bkr.at[d], b1_s.at[w], b1_r.at[d], w, s)

    def head_stage(q):
        p = pair_of(q)
        parts = []
        for u in range(2):
            w = window(p, u)

            def arrive():
                send(hid.at[w], hid.at[w], hid_s.at[0], hid_r.at[w], sib, s).wait_recv()

            def arrive_aux():
                send(aux.at[w], aux.at[w], aux_s.at[0], aux_r.at[w], sib, s).wait_recv()

            if u == 0:

                if relay:

                    @pl.when(q == 1)
                    def _():
                        for k in (1, 2):
                            v = 2 * pair_of(k) + core
                            send(
                                hid.at[v], hid.at[v], hid_s.at[0], hid_r.at[v], sib, s
                            ).wait_recv()
                            relay_copy(k).start()
                            forward(v).start()

                    @pl.when(q == 3)
                    def _():
                        relay_wait(1)
                        relay_wait(2)
                        forward(w).start()

                else:

                    @pl.when(q > 0)
                    def _():
                        arrive()
                        forward(w).start()

                pl.when(q > 0)(arrive_aux)

            else:
                arrive()
                arrive_aux()
            out = mm(hid[w], w_vm[...])
            out += mm_tn(aux[w, 0:rank], up[...])
            out += bias[...]
            e = jnp.exp(-jnp.abs(out))
            r = 1.0 / (1.0 + e)
            sig[w] = jnp.where(out >= 0, r, e * r)
            predicted = jnp.maximum(out, 0.0) + jnp.log1p(e)
            high = predicted.astype(BF16)
            low = (predicted - high.astype(F32)).astype(BF16)
            mem = aux[w, rank : rank + genes]
            parts.append(mm(mem, high) + mm(mem, low))
        for j in range(m):
            covp[p, j] = jnp.concatenate(
                [part[j * owned : (j + 1) * owned] for part in parts], axis=0
            )
        covr[p, s] = covp[p, s]
        for k in range(1, m):
            cov_copy(p, seq_peer(k)).start()

    def slope_stage(q):
        p = pair_of(q)
        for k in range(1, m):
            j = seq_peer(k)
            send(covr.at[p, j], covr.at[p, j], cov_s.at[p, j], cov_r.at[p, j], d, j).wait_recv()
        total = covr[p, 0]
        for j in range(1, m):
            total += covr[p, j]
        covt[p] = total
        wants = []
        for u in range(2):
            t8 = tgt[window(p, u)].astype(F32)
            want = t8[0:owned]
            for i in range(1, 8 // owned):
                want = jnp.where(
                    (s * owned) % 8 == i * owned, t8[i * owned : (i + 1) * owned], want
                )
            wants.append(want)
        want = jnp.concatenate(wants, axis=0)
        acc[rank + 8 :] += total - want * jnp.log1p(total)
        slp[p, s] = scale * (1.0 - want / (1.0 + total))
        for k in range(1, m):
            slp_copy(p, k).start()

        @pl.when(q > 0)
        def _():
            out_copy(p, window(p, 0)).start()

        out_copy(p, window(p, 1)).start()

    def grad_stage(q):
        p = pair_of(q)
        for k in range(1, m):
            j = seq_peer(k)
            send(slp.at[p, j], slp.at[p, j], slp_s.at[p, k], slp_r.at[p, j], d, j).wait_recv()
        for u in range(2):
            w = window(p, u)
            slopes = jnp.concatenate(
                [slp[p, j][u * owned : (u + 1) * owned] for j in range(m)], axis=0
            )
            s0 = slopes.astype(BF16)
            left = slopes - s0.astype(F32)
            s1 = left.astype(BF16)
            s2 = (left - s1.astype(F32)).astype(BF16)
            mem = aux[w, rank : rank + genes]
            spread = mm_tn(
                jnp.concatenate([mem, mem, mem], axis=0), jnp.concatenate([s0, s1, s2], axis=0)
            )
            grad = spread * sig[w]
            half = grad.astype(BF16)
            acc[0:rank] += mm(aux[w, 0:rank], half)
            acc[rank : rank + 8] += jnp.sum(grad.reshape(rows // 8, 8, cols), axis=0)
            bkp[w] = mm_nt(up[...], half)
            if u == 0:

                @pl.when(q == 0)
                def _():
                    bkr[d] = bkp[d]

                @pl.when(q > 0)
                def _():
                    back_copy(w).start()

            else:
                back_copy(w).start()

    def step(q, carry):
        @pl.when(q < nc)
        def _():
            head_stage(q)

        @pl.when((q >= 1) & (q < nc + 1))
        def _():
            slope_stage(q - 1)

        @pl.when(q >= 2)
        def _():
            grad_stage(q - 2)

        return carry

    lax.fori_loop(0, nc + 2, step, 0)

    ups[s, 0:rank] = acc[0:rank]
    ups[s, rank : rank + 8] = jnp.concatenate(
        [
            jnp.sum(acc[rank : rank + 8], axis=0, keepdims=True),
            scale * jnp.sum(acc[rank + 8 :], axis=0, keepdims=True),
            jnp.zeros((6, cols), F32),
        ],
        axis=0,
    )
    up_copies = []
    for k in range(1, m):
        c = send(ups.at[s], ups.at[s], us_s.at[k], us_r.at[s], d, seq_peer(k))
        c.start()
        up_copies.append(c)

    for k in range(1, n):
        j = dp_peer(k)
        send(bkr.at[j], bkr.at[j], b1_s.at[j], b1_r.at[j], j, s).wait_recv()
    total = bkr[0]
    for j in range(1, n):
        total += bkr[j]
    bk[d] = total.astype(BF16)
    bk_copies = []
    for k in range(1, n):
        c = send(bk.at[d], bk.at[d], b2_s.at[k], b2_r.at[d], dp_peer(k), s)
        c.start()
        bk_copies.append(c)

    for k in range(1, m):
        j = seq_peer(k)
        send(ups.at[j], ups.at[j], us_s.at[k], us_r.at[j], d, j).wait_recv()
    total = ups[0]
    for j in range(1, m):
        total += ups[j]
    fin[d] = total
    fin_copies = []
    for k in range(1, n):
        c = send(fin.at[d], fin.at[d], fu_s.at[k], fu_r.at[d], dp_peer(k), s)
        c.start()
        fin_copies.append(c)

    for k in range(1, n):
        j = dp_peer(k)
        send(bk.at[j], bk.at[j], b2_s.at[k], b2_r.at[j], j, s).wait_recv()
    part = d % PARTS
    lanes = pl.ds(pl.multiple_of(part * wide, 128), wide)
    group = (d // PARTS) * PARTS

    def down_step(w, total):
        return total + mm(bk[w], hid[w, :, lanes])

    dns[s] = lax.fori_loop(0, n, down_step, jnp.zeros((rank, wide), F32))
    dn_copies = []
    for k in range(1, m):
        c = send(dns.at[s], dns.at[s], ds_s.at[k], ds_r.at[s], d, seq_peer(k))
        c.start()
        dn_copies.append(c)

    covin[d] = covt[chip]
    for k in range(1, n):
        j = dp_peer(k)
        send(covin.at[j], covin.at[j], co_s.at[k], co_r.at[j], j, s).wait_recv()
    for j in range(n):
        both = covin[j]
        cov_out[0, :, j * cols : (j + 1) * cols] = jnp.where(
            core == j % 2, both[0:owned], both[owned : 2 * owned]
        )

    for k in range(1, m):
        j = seq_peer(k)
        send(dns.at[j], dns.at[j], ds_s.at[k], ds_r.at[j], d, j).wait_recv()
    total = dns[0]
    for j in range(1, m):
        total += dns[j]
    dnf[part] = total
    for k in range(1, PARTS):
        c = send(
            dnf.at[part], dnf.at[part], fd_s.at[k], fd_r.at[part], group + (part + k) % PARTS, s
        )
        c.start()
        fin_copies.append(c)

    for k in range(1, n):
        j = dp_peer(k)
        send(fin.at[j], fin.at[j], fu_s.at[k], fu_r.at[j], j, s).wait_recv()
    loss = jnp.zeros((1, cols), F32)
    for j in range(n):
        up_out[:, j * cols : (j + 1) * cols] = fin[j, 0:rank]
        bias_out[:, j * cols : (j + 1) * cols] = fin[j, rank : rank + 1]
        loss += fin[j, rank + 1 : rank + 2]
    loss_out[...] = jnp.sum(loss, axis=1, keepdims=True)

    for k in range(1, PARTS):
        j = (part + k) % PARTS
        send(dnf.at[j], dnf.at[j], fd_s.at[k], fd_r.at[j], group + j, s).wait_recv()
    for j in range(PARTS):
        down_out[:, j * wide : (j + 1) * wide] = dnf[j]

    @pl.when(s < m - 1)
    def _():
        to_next.wait_send()

    @pl.when(s > 0)
    def _():
        to_prev.wait_send()

    for c in (
        bin_copies
        + tgt_copies
        + hid_copies
        + aux_copies
        + up_copies
        + bk_copies
        + dn_copies
        + fin_copies
    ):
        c.wait_send()

    if relay:
        for k in (1, 2):
            relay_copy(k).wait_send()

    def drain(q, carry):
        p = pair_of(q)
        for k in range(1, m):
            cov_copy(p, seq_peer(k)).wait_send()
            slp_copy(p, k).wait_send()

        @pl.when(q > 0)
        def _():
            forward(window(p, 0)).wait_send()
            back_copy(window(p, 0)).wait_send()
            out_copy(p, window(p, 0)).wait_send()

        out_copy(p, window(p, 1)).wait_send()
        back_copy(window(p, 1)).wait_send()
        return carry

    lax.fori_loop(0, nc, drain, 0)


def emit(*refs):
    sems = refs[-1]
    k = (len(refs) - 1) // 2
    copies = [
        pltpu.make_async_copy(refs[i], refs[k + i], sems.at[i]) for i in range(k)
    ]
    for c in copies:
        c.start()
    for c in copies:
        c.wait()


def local(
    n,
    m,
    coarse,
    skip_feats,
    conv_taps,
    norm_gain,
    head_weight,
    adapter_down,
    adapter_up,
    head_bias,
    exon_bins,
    exon_count,
    targets,
):
    rows, chans = skip_feats.shape[1:]
    cols = head_weight.shape[1]
    tracks = adapter_up.shape[1]
    rank = adapter_up.shape[0]
    owned = exon_bins.shape[1]
    genes = owned * m
    nc = n // 2
    wide = chans // PARTS
    scale = 1.0 / (n * genes)
    vm = pl.BlockSpec(memory_space=pltpu.VMEM)
    hbm = pl.BlockSpec(memory_space=pltpu.HBM)
    dma = pltpu.SemaphoreType.DMA
    cov, loss, down, up, bias = pl.pallas_call(
        functools.partial(kernel, n, m, scale),
        out_shape=(
            pltpu.VMEM((1, owned, tracks), F32),
            pltpu.VMEM((1, 1), F32),
            pltpu.VMEM((rank, chans), F32),
            pltpu.VMEM((rank, tracks), F32),
            pltpu.VMEM((1, tracks), F32),
        ),
        in_specs=[hbm] * 11,
        out_specs=(vm,) * 5,
        scratch_shapes=[
            pltpu.VMEM((1, rows // 2, chans), BF16),
            pltpu.VMEM((1, rows, chans), BF16),
            pltpu.VMEM(conv_taps.shape, F32),
            pltpu.VMEM((chans,), F32),
            pltpu.VMEM((rank, chans), BF16),
            pltpu.VMEM((rank, cols), BF16),
            pltpu.VMEM((1, cols), F32),
            pltpu.VMEM(exon_bins.shape, jnp.int32),
            pltpu.VMEM(exon_count.shape, jnp.int32),
            pltpu.VMEM((chans, cols), BF16),
            pltpu.VMEM((n, rows, chans), BF16),
            pltpu.VMEM((n, rank + genes, rows), BF16),
            pltpu.VMEM((2, 1, chans), F32),
            pltpu.VMEM((2, 1, chans), F32),
            pltpu.VMEM((m, 8, 128), jnp.int32),
            pltpu.VMEM((n, 8, cols), jnp.int32),
            pltpu.VMEM((n, rows, cols), F32),
            pltpu.VMEM((nc, m, 2 * owned, cols), F32),
            pltpu.VMEM((nc, m, 2 * owned, cols), F32),
            pltpu.VMEM((nc, 2 * owned, cols), F32),
            pltpu.VMEM((nc, m, 2 * owned, cols), F32),
            pltpu.VMEM((n, 2 * owned, cols), F32),
            pltpu.VMEM((n, rank, rows), F32),
            pltpu.VMEM((n, rank, rows), F32),
            pltpu.VMEM((n, rank, rows), BF16),
            pltpu.VMEM((rank + 16, cols), F32),
            pltpu.VMEM((m, rank + 8, cols), F32),
            pltpu.VMEM((m, rank, wide), F32),
            pltpu.VMEM((n, rank + 8, cols), F32),
            pltpu.VMEM((PARTS, rank, wide), F32),
            dma((12,)),
            dma((2,)),
            dma((2,)),
            dma((m,)),
            dma((m,)),
            dma((2,)),
            dma((2,)),
            dma((n,)),
            dma((n,)),
            dma((n,)),
            dma((n,)),
            dma((n,)),
            dma((n,)),
            dma((n,)),
            dma((nc, m)),
            dma((nc, m)),
            dma((nc, m)),
            dma((nc, m)),
            dma((n,)),
            dma((n,)),
            dma((n,)),
            dma((n,)),
            dma((n,)),
            dma((n,)),
            dma((m,)),
            dma((m,)),
            dma((m,)),
            dma((m,)),
            dma((n,)),
            dma((n,)),
            dma((PARTS,)),
            dma((PARTS,)),
        ],
        compiler_params=pltpu.CompilerParams(
            collective_id=0, has_side_effects=True, vmem_limit_bytes=56 * 2**20
        ),
    )(
        coarse,
        skip_feats,
        conv_taps,
        norm_gain,
        head_weight,
        adapter_down.T,
        adapter_up,
        head_bias.reshape(1, tracks),
        exon_bins,
        exon_count,
        targets,
    )
    held = (cov, loss, down, up, bias)
    cov, loss, down, up, bias = pl.pallas_call(
        emit,
        in_specs=[vm] * 5,
        out_shape=tuple(jax.ShapeDtypeStruct(a.shape, a.dtype) for a in held),
        out_specs=(hbm,) * 5,
        scratch_shapes=[dma((5,))],
    )(*[pltpu.with_memory_space_constraint(h, pltpu.VMEM) for h in held])
    return cov, loss[0, 0], down.T, up, bias.reshape(tracks)


def solution(mesh):
    placed = (
        P("dp", "seq", None),
        P("dp", "seq", None),
        P(),
        P(),
        P(None, "dp"),
        P(),
        P(),
        P(),
        P("dp", "seq", None),
        P("dp", "seq"),
        P("dp", None, None),
    )
    return jax.shard_map(
        functools.partial(local, mesh.shape["dp"], mesh.shape["seq"]),
        mesh=mesh,
        in_specs=placed,
        out_specs=(P("dp", "seq", None), P(), P(), P(), P()),
        check_vma=False,
    )
```

```python
import functools

import jax
import jax.numpy as jnp
from jax import lax
from jax.experimental import pallas as pl
from jax.experimental.pallas import tpu as pltpu
from jax.sharding import PartitionSpec as P

MESH = pl.DeviceIdType.MESH
F32 = jnp.float32
BF16 = jnp.bfloat16
CHUNKS = 8
EDGE = 16


def mm(a, b):
    return jnp.dot(a, b, preferred_element_type=F32)


def mm_nt(a, b):
    return lax.dot_general(a, b, (((1,), (1,)), ((), ())), preferred_element_type=F32)


def mm_tn(a, b):
    return lax.dot_general(a, b, (((0,), (0,)), ((), ())), preferred_element_type=F32)


def kernel(
    n,
    m,
    scale,
    coarse_h,
    skip_h,
    taps_h,
    gain_h,
    weight,
    down_h,
    up_h,
    bias_h,
    bins_h,
    count_h,
    targets,
    cov_out,
    loss_out,
    down_out,
    up_out,
    bias_out,
    coarse,
    skip,
    taps,
    gain,
    down,
    up,
    bias,
    bins,
    count,
    w_vm,
    tfull,
    hid,
    aux,
    halo,
    edge,
    binbuf,
    tsel,
    tgt,
    sig,
    covp,
    covr,
    covt,
    slp,
    covin,
    acc,
    bkc,
    dn,
    dnr,
    dnz,
    dnf,
    ups,
    fin,
    sem_loc,
    halo_s,
    halo_r,
    bin_s,
    bin_r,
    relay_s,
    hid_s,
    fwd_s,
    hid_r,
    aux_s,
    aux_r,
    tgt_s,
    tgt_r,
    cov_s,
    cov_r,
    slp_s,
    slp_r,
    co_s,
    co_r,
    us_s,
    us_r,
    fu_s,
    fu_r,
    ds_s,
    ds_r,
    dz_s,
    dz_r,
    fd_s,
    fd_r,
):
    d = lax.axis_index("dp")
    s = lax.axis_index("seq")
    nc = n // 2
    relay = nc == 4
    chip = d // 2
    core = d % 2
    sib = chip * 2 + (1 - core)
    rows, chans = skip.shape[1], skip.shape[2]
    cols = weight.shape[1]
    owned = bins.shape[1]
    slots = bins.shape[2]
    rank = up.shape[0]
    genes = owned * m
    inner = rows - 2 * EDGE
    mid = inner // 2
    lines = cols // 128
    wide = chans // (CHUNKS // 2)
    tall = rank // 2

    def pair_of(q):
        found, bit = 0, 1
        while bit < nc:
            found = found + bit * (((chip // bit) % 2 + (q // bit) % 2) % 2)
            bit *= 2
        return found

    def send(src, dst, ss, rs, dd, jj):
        return pltpu.make_async_remote_copy(
            src_ref=src,
            dst_ref=dst,
            send_sem=ss,
            recv_sem=rs,
            device_id=(dd, jj),
            device_id_type=MESH,
        )

    def dp_peer(k):
        return (d + k) % n

    def seq_peer(k):
        return (s + k) % m

    def column(k):
        return pl.ds(pl.multiple_of(k * cols, 128), cols)

    tile = 8 * (s * owned // 8)
    loads = []
    for src, dst in (
        (skip_h, skip),
        (coarse_h, coarse),
        (taps_h, taps),
        (gain_h, gain),
        (bins_h, bins),
        (count_h, count),
        (down_h, down),
        (targets.at[0, pl.ds(pl.multiple_of(tile, 8), 8)], tfull),
        (up_h.at[:, column(d)], up),
        (bias_h.at[:, column(d)], bias),
        (weight, w_vm),
    ):
        c = pltpu.make_async_copy(src, dst, sem_loc.at[len(loads)])
        c.start()
        loads.append(c)
    barrier = pltpu.get_barrier_semaphore()
    for k in range(1, m):
        pl.semaphore_signal(barrier, inc=1, device_id=(d, seq_peer(k)), device_id_type=MESH)
    for k in range(1, n):
        pl.semaphore_signal(barrier, inc=1, device_id=(dp_peer(k), s), device_id_type=MESH)

    for c in loads[:2]:
        c.wait()
    rr = lax.broadcasted_iota(jnp.int32, (rows, rows // 2), 0)
    cc = lax.broadcasted_iota(jnp.int32, (rows, rows // 2), 1)
    spread2 = jnp.where(rr // 2 == cc, 1.0, 0.0).astype(BF16)
    merged = (mm(spread2, coarse[0]) + skip[0].astype(F32)).astype(BF16).astype(F32)
    edge[0] = merged[0:1]
    edge[1] = merged[rows - 1 : rows]

    for c in loads[2:6]:
        c.wait()

    def activate(before, at, after):
        mixed = taps[0:1] * before + taps[1:2] * at + taps[2:3] * after
        normed = (
            mixed
            * lax.rsqrt(jnp.mean(mixed * mixed, axis=-1, keepdims=True) + 1e-06)
            * gain[...].reshape(1, chans)
        )
        return jax.nn.gelu(normed).astype(BF16)

    hid[d, 0:inner] = activate(
        pltpu.roll(merged, 1, 0)[EDGE : rows - EDGE],
        merged[EDGE : rows - EDGE],
        pltpu.roll(merged, rows - 1, 0)[EDGE : rows - EDGE],
    )

    cnt = jnp.broadcast_to(count[...].astype(F32), (owned, owned))
    er = lax.broadcasted_iota(jnp.int32, (owned, owned), 0)
    ec = lax.broadcasted_iota(jnp.int32, (owned, owned), 1)
    cnt = jnp.sum(jnp.where(er == ec, cnt, 0.0), axis=1, keepdims=True)
    slot = lax.broadcasted_iota(jnp.int32, (owned, slots), 1).astype(F32)
    binbuf[s] = jnp.full((8, 128), -1, jnp.int32)
    binbuf[s, 0:owned, 0:slots] = jnp.where(slot < cnt, bins[0], -1)

    first, second = pl.ds(0, mid), pl.ds(mid, mid)
    whole, rim = pl.ds(0, inner), pl.ds(inner, 2 * EDGE)
    rims = (pl.ds(inner, EDGE), pl.ds(inner + EDGE, EDGE))

    def block_copy(w, part, sem, lane, to):
        return send(hid.at[w, part], hid.at[w, part], sem, hid_r.at[w, lane], to, s)

    def own_copy(k, part, lane):
        to = sib if k == 0 else pair_of(k) * 2 + core
        return block_copy(d, part, hid_s.at[k, lane], lane, to)

    def forward(w, part, lane):
        return block_copy(w, part, fwd_s.at[w, lane], lane, sib)

    def arrive(w, part, lane):
        block_copy(w, part, hid_s.at[0, lane], lane, sib).wait_recv()

    def relay_copy(k, lane):
        w = 2 * pair_of(k) + core
        part = ((first, second)[k - 1], rims[k - 1])[lane]
        there = 2 * pair_of(3 - k) + core
        return block_copy(w, part, relay_s.at[k - 1, lane], 2 * lane + k - 1, there)

    pl.semaphore_wait(barrier, n + m - 2)

    to_next = send(edge.at[1], halo.at[0], halo_s.at[0], halo_r.at[0], d, (s + 1) % m)
    to_prev = send(edge.at[0], halo.at[1], halo_s.at[1], halo_r.at[1], d, (s + m - 1) % m)

    @pl.when(s < m - 1)
    def _():
        to_next.start()

    @pl.when(s > 0)
    def _():
        to_prev.start()

    hid_copies = []

    def start(c):
        c.start()
        hid_copies.append(c)

    if relay:
        start(own_copy(1, first, 0))
        start(own_copy(2, second, 1))
        start(own_copy(1, second, 1))
        start(own_copy(2, first, 0))
    else:
        for k in range(1, nc):
            start(own_copy(k, whole, 0))
    start(own_copy(0, whole, 0))

    bin_copies = []
    for k in range(1, m):
        c = send(binbuf.at[s], binbuf.at[s], bin_s.at[k], bin_r.at[s], d, seq_peer(k))
        c.start()
        bin_copies.append(c)

    @pl.when(s == 0)
    def _():
        halo[0] = jnp.zeros((1, chans), F32)

    @pl.when(s == m - 1)
    def _():
        halo[1] = jnp.zeros((1, chans), F32)

    for c in loads[6:8]:
        c.wait()
    t8 = tfull[...]
    want = t8[0:owned]
    for i in range(1, 8 // owned):
        want = jnp.where((s * owned) % 8 == i * owned, t8[i * owned : (i + 1) * owned], want)
    for j in range(n):
        tsel[j] = want[:, j * cols : (j + 1) * cols]
    tgt[d] = tsel[d]
    acc[...] = jnp.zeros(acc.shape, F32)
    dn[...] = jnp.zeros(dn.shape, F32)

    @pl.when(s > 0)
    def _():
        to_next.wait_recv()

    @pl.when(s < m - 1)
    def _():
        to_prev.wait_recv()

    reach = EDGE + 8
    row = lax.broadcasted_iota(jnp.int32, (reach, chans), 0)
    top, low = merged[0:reach], merged[rows - reach :]
    hid[d, inner + EDGE :] = activate(
        jnp.where(row == 0, halo[0], pltpu.roll(top, 1, 0))[0:EDGE],
        top[0:EDGE],
        pltpu.roll(top, reach - 1, 0)[0:EDGE],
    )
    hid[d, inner : inner + EDGE] = activate(
        pltpu.roll(low, 1, 0)[8:],
        low[8:],
        jnp.where(row == reach - 1, halo[1], pltpu.roll(low, reach - 1, 0))[8:],
    )
    for k in range(1, 3 if relay else nc):
        start(own_copy(k, rim, 2))
    start(own_copy(0, rim, 2))

    aux[d, 0:rank] = mm_nt(down[...], hid[d]).astype(BF16)

    for k in range(1, m):
        j = seq_peer(k)
        send(binbuf.at[j], binbuf.at[j], bin_s.at[k], bin_r.at[j], d, j).wait_recv()
    listed = jnp.concatenate([binbuf[j][0:owned] for j in range(m)], axis=0)
    here = s * rows + (lax.broadcasted_iota(jnp.int32, (genes, rows), 1) + EDGE) % rows
    member = jnp.zeros((genes, rows), F32)
    for j in range(slots):
        member += jnp.where(listed[:, j : j + 1] == here, 1.0, 0.0)
    aux[d, rank : rank + genes] = member.astype(BF16)

    aux_copies = []
    for k in range(1, n):
        c = send(aux.at[d], aux.at[d], aux_s.at[k], aux_r.at[d], dp_peer(k), s)
        c.start()
        aux_copies.append(c)

    tgt_copies = []
    for k in range(1, n):
        j = dp_peer(k)
        c = send(tsel.at[j], tgt.at[d], tgt_s.at[k], tgt_r.at[d], j, s)
        c.start()
        tgt_copies.append(c)

    for c in loads[8:]:
        c.wait()

    def window(p, u):
        return 2 * p + (core if u == 0 else 1 - core)

    def cov_copy(p, j):
        return send(covp.at[p, j], covr.at[p, s], cov_s.at[p, j], cov_r.at[p, s], d, j)

    def slp_copy(p, k):
        return send(slp.at[p, s], slp.at[p, s], slp_s.at[p, k], slp_r.at[p, s], d, seq_peer(k))

    def out_copy(p, w):
        return send(covt.at[p], covin.at[d], co_s.at[w], co_r.at[d], w, s)

    def head_stage(q):
        p = pair_of(q)
        parts = []
        for u in range(2):
            w = window(p, u)

            def arrive_aux():
                send(aux.at[w], aux.at[w], aux_s.at[0], aux_r.at[w], sib, s).wait_recv()

            if u == 0:
                if relay:

                    @pl.when(q == 1)
                    def _():
                        near = [2 * pair_of(k) + core for k in (1, 2)]
                        arrive(near[0], second, 1)
                        forward(near[0], whole, 0).start()
                        arrive(near[1], first, 0)
                        forward(near[1], whole, 0).start()
                        for k in (1, 2):
                            arrive(near[k - 1], rim, 2)
                            relay_copy(k, 1).start()
                            forward(near[k - 1], rim, 2).start()

                    @pl.when(q == 3)
                    def _():
                        arrive(w, first, 0)
                        forward(w, first, 0).start()
                        arrive(w, second, 1)
                        forward(w, second, 1).start()
                        arrive(w, rims[0], 2)
                        arrive(w, rims[1], 3)
                        forward(w, rim, 2).start()

                else:

                    @pl.when(q > 0)
                    def _():
                        arrive(w, whole, 0)
                        forward(w, whole, 0).start()
                        arrive(w, rim, 2)
                        forward(w, rim, 2).start()

                pl.when(q > 0)(arrive_aux)

            else:
                if relay:

                    @pl.when(q == 0)
                    def _():
                        arrive(2 * pair_of(1) + core, first, 0)
                        relay_copy(1, 0).start()
                        arrive(2 * pair_of(2) + core, second, 1)
                        relay_copy(2, 0).start()

                    @pl.when(q < 3)
                    def _():
                        arrive(w, whole, 0)

                    @pl.when(q == 3)
                    def _():
                        arrive(w, first, 0)
                        arrive(w, second, 1)

                else:
                    arrive(w, whole, 0)
                arrive(w, rim, 2)
                arrive_aux()
            out = mm(hid[w], w_vm[...])
            out += mm_tn(aux[w, 0:rank], up[...])
            out += bias[...]
            e = jnp.exp(-jnp.abs(out))
            r = 1.0 / (1.0 + e)
            sig[w] = jnp.where(out >= 0, r, e * r)
            predicted = jnp.maximum(out, 0.0) + jnp.log1p(e)
            high = predicted.astype(BF16)
            low = (predicted - high.astype(F32)).astype(BF16)
            mem = aux[w, rank : rank + genes]
            parts.append(mm(mem, high) + mm(mem, low))
        for j in range(m):
            covp[p, j] = jnp.concatenate(
                [part[j * owned : (j + 1) * owned] for part in parts], axis=0
            )
        covr[p, s] = covp[p, s]
        for k in range(1, m):
            cov_copy(p, seq_peer(k)).start()

    def slope_stage(q):
        p = pair_of(q)
        wants = []
        for u in range(2):
            w = window(p, u)

            def arrive_tgt():
                send(tgt.at[w], tgt.at[w], tgt_s.at[0], tgt_r.at[w], sib, s).wait_recv()

            if u == 0:
                pl.when(q > 0)(arrive_tgt)
            else:
                arrive_tgt()
            wants.append(tgt[w].astype(F32))
        want = jnp.concatenate(wants, axis=0)
        for k in range(1, m):
            j = seq_peer(k)
            send(covr.at[p, j], covr.at[p, j], cov_s.at[p, j], cov_r.at[p, j], d, j).wait_recv()
        total = covr[p, 0]
        for j in range(1, m):
            total += covr[p, j]
        slp[p, s] = scale * (1.0 - want / (1.0 + total))
        for k in range(1, m):
            slp_copy(p, k).start()
        covt[p] = total
        acc[rank + 8 :] += total - want * jnp.log1p(total)

        @pl.when(q > 0)
        def _():
            out_copy(p, window(p, 0)).start()

        out_copy(p, window(p, 1)).start()

    def grad_stage(q):
        p = pair_of(q)
        for k in range(1, m):
            j = seq_peer(k)
            send(slp.at[p, j], slp.at[p, j], slp_s.at[p, k], slp_r.at[p, j], d, j).wait_recv()
        for u in range(2):
            w = window(p, u)
            slopes = jnp.concatenate(
                [slp[p, j][u * owned : (u + 1) * owned] for j in range(m)], axis=0
            )
            s0 = slopes.astype(BF16)
            left = slopes - s0.astype(F32)
            s1 = left.astype(BF16)
            s2 = (left - s1.astype(F32)).astype(BF16)
            mem = aux[w, rank : rank + genes]
            spread = mm_tn(
                jnp.concatenate([mem, mem, mem], axis=0), jnp.concatenate([s0, s1, s2], axis=0)
            )
            grad = spread * sig[w]
            half = grad.astype(BF16)
            acc[0:rank] += mm(aux[w, 0:rank], half)
            acc[rank : rank + 8] += jnp.sum(grad.reshape(rows // 8, 8, cols), axis=0)
            back = mm_nt(up[...], half)
            high = back.astype(BF16)
            low = (back - high.astype(F32)).astype(BF16)
            side = core if u == 0 else 1 - core
            bkc[:, pl.ds(pl.multiple_of(side * rows, 128), rows)] = jnp.concatenate(
                [high, low], axis=0
            )
        both = mm(bkc[...], hid[pl.ds(2 * p, 2)].reshape(2 * rows, chans))
        both = both[0:rank] + both[rank:]
        for k in range(CHUNKS):
            y, x = (k % 2) * tall, (k // 2) * wide
            dn[k] += both[y : y + tall, x : x + wide]

    def step(q, carry):
        @pl.when(q < nc)
        def _():
            head_stage(q)

        @pl.when((q >= 1) & (q < nc + 1))
        def _():
            slope_stage(q - 1)

        @pl.when(q >= 2)
        def _():
            grad_stage(q - 2)

        return carry

    lax.fori_loop(0, nc + 2, step, 0)

    ups[s, :, 0:cols] = acc[0:rank]
    bias_sum = jnp.sum(acc[rank : rank + 8], axis=0, keepdims=True)
    loss_sum = scale * jnp.sum(acc[rank + 8 :], axis=0, keepdims=True)
    small = [bias_sum[:, i * 128 : (i + 1) * 128] for i in range(lines)]
    small += [loss_sum[:, i * 128 : (i + 1) * 128] for i in range(lines)]
    if rank > 2 * lines:
        small.append(jnp.zeros((rank - 2 * lines, 128), F32))
    ups[s, :, cols:] = jnp.concatenate(small, axis=0)
    up_copies = []
    for k in range(1, m):
        c = send(ups.at[s], ups.at[s], us_s.at[k], us_r.at[s], d, seq_peer(k))
        c.start()
        up_copies.append(c)

    def part_copy(j):
        return send(dn.at[j], dnr.at[d], ds_s.at[j], ds_r.at[d], j, s)

    def if_owner(f):
        if n > CHUNKS:
            pl.when(d < CHUNKS)(f)
        else:
            f()

    def if_other(j, f):
        pl.when(d != j)(f)

    for j in range(CHUNKS):
        if_other(j, lambda: part_copy(j).start())

    covin[d] = covt[chip]
    for k in range(1, n):
        j = dp_peer(k)
        send(covin.at[j], covin.at[j], co_s.at[k], co_r.at[j], j, s).wait_recv()
    for j in range(n):
        both = covin[j]
        cov_out[0, :, j * cols : (j + 1) * cols] = jnp.where(
            core == j % 2, both[0:owned], both[owned : 2 * owned]
        )

    @pl.when(s < m - 1)
    def _():
        to_next.wait_send()

    @pl.when(s > 0)
    def _():
        to_prev.wait_send()

    for c in bin_copies + tgt_copies + hid_copies + aux_copies:
        c.wait_send()

    if relay:
        for k in (1, 2):
            for lane in (0, 1):
                relay_copy(k, lane).wait_send()

    def drain(q, carry):
        p = pair_of(q)
        for k in range(1, m):
            cov_copy(p, seq_peer(k)).wait_send()
            slp_copy(p, k).wait_send()

        @pl.when(q > 0)
        def _():
            w = window(p, 0)
            if relay:

                @pl.when(q < 3)
                def _():
                    forward(w, whole, 0).wait_send()

                @pl.when(q == 3)
                def _():
                    forward(w, first, 0).wait_send()
                    forward(w, second, 1).wait_send()

            else:
                forward(w, whole, 0).wait_send()
            forward(w, rim, 2).wait_send()
            out_copy(p, w).wait_send()

        out_copy(p, window(p, 1)).wait_send()
        return carry

    lax.fori_loop(0, nc, drain, 0)

    def gathered_z(k):
        j = seq_peer(k)
        return send(dnz.at[s], dnz.at[s], dz_s.at[k], dz_r.at[s], d, j)

    def spread_part(k):
        return send(dnf.at[d], dnf.at[d], fd_s.at[k], fd_r.at[d], dp_peer(k), s)

    def sum_plane():
        dnr[d] = dn[d]
        for k in range(1, n):
            j = dp_peer(k)
            send(dnr.at[j], dnr.at[j], ds_s.at[0], ds_r.at[j], j, s).wait_recv()
        total = dnr[0]
        for j in range(1, n):
            total += dnr[j]
        dnz[s] = total
        for k in range(1, m):
            gathered_z(k).start()

    if_owner(sum_plane)

    for k in range(1, m):
        j = seq_peer(k)
        send(ups.at[j], ups.at[j], us_s.at[k], us_r.at[j], d, j).wait_recv()
    total = ups[0]
    for j in range(1, m):
        total += ups[j]
    fin[d] = total
    fin_copies = []
    for k in range(1, n):
        c = send(fin.at[d], fin.at[d], fu_s.at[k], fu_r.at[d], dp_peer(k), s)
        c.start()
        fin_copies.append(c)

    def sum_seq():
        for k in range(1, m):
            j = seq_peer(k)
            send(dnz.at[j], dnz.at[j], dz_s.at[k], dz_r.at[j], d, j).wait_recv()
        total = dnz[0]
        for j in range(1, m):
            total += dnz[j]
        dnf[d] = total
        for k in range(1, n):
            spread_part(k).start()

    if_owner(sum_seq)

    for c in up_copies:
        c.wait_send()
    for j in range(CHUNKS):
        if_other(j, lambda: part_copy(j).wait_send())

    def drain_z():
        for k in range(1, m):
            gathered_z(k).wait_send()

    if_owner(drain_z)

    for k in range(1, n):
        j = dp_peer(k)
        send(fin.at[j], fin.at[j], fu_s.at[k], fu_r.at[j], j, s).wait_recv()
    loss = jnp.zeros((lines, 128), F32)
    for j in range(n):
        up_out[:, j * cols : (j + 1) * cols] = fin[j, :, 0:cols]
        for i in range(lines):
            x = j * cols + i * 128
            bias_out[:, x : x + 128] = fin[j, i : i + 1, cols:]
        loss += fin[j, lines : 2 * lines, cols:]
    loss_out[...] = jnp.sum(jnp.sum(loss, axis=0, keepdims=True), axis=1, keepdims=True)

    for j in range(CHUNKS):

        def arrive_part():
            send(dnf.at[j], dnf.at[j], fd_s.at[0], fd_r.at[j], j, s).wait_recv()

        if_other(j, arrive_part)
        y, x = (j % 2) * tall, (j // 2) * wide
        down_out[y : y + tall, x : x + wide] = dnf[j]

    for c in fin_copies:
        c.wait_send()

    def drain_parts():
        for k in range(1, n):
            spread_part(k).wait_send()

    if_owner(drain_parts)


def emit(*refs):
    sems = refs[-1]
    k = (len(refs) - 1) // 2
    copies = [
        pltpu.make_async_copy(refs[i], refs[k + i], sems.at[i]) for i in range(k)
    ]
    for c in copies:
        c.start()
    for c in copies:
        c.wait()


def local(
    n,
    m,
    coarse,
    skip_feats,
    conv_taps,
    norm_gain,
    head_weight,
    adapter_down,
    adapter_up,
    head_bias,
    exon_bins,
    exon_count,
    targets,
):
    rows, chans = skip_feats.shape[1:]
    cols = head_weight.shape[1]
    tracks = adapter_up.shape[1]
    rank = adapter_up.shape[0]
    owned = exon_bins.shape[1]
    genes = owned * m
    nc = n // 2
    wide = chans // (CHUNKS // 2)
    scale = 1.0 / (n * genes)
    vm = pl.BlockSpec(memory_space=pltpu.VMEM)
    hbm = pl.BlockSpec(memory_space=pltpu.HBM)
    dma = pltpu.SemaphoreType.DMA
    cov, loss, down, up, bias = pl.pallas_call(
        functools.partial(kernel, n, m, scale),
        out_shape=(
            pltpu.VMEM((1, owned, tracks), F32),
            pltpu.VMEM((1, 1), F32),
            pltpu.VMEM((rank, chans), F32),
            pltpu.VMEM((rank, tracks), F32),
            pltpu.VMEM((1, tracks), F32),
        ),
        in_specs=[hbm] * 11,
        out_specs=(vm,) * 5,
        scratch_shapes=[
            pltpu.VMEM((1, rows // 2, chans), BF16),
            pltpu.VMEM((1, rows, chans), BF16),
            pltpu.VMEM(conv_taps.shape, F32),
            pltpu.VMEM((chans,), F32),
            pltpu.VMEM((rank, chans), BF16),
            pltpu.VMEM((rank, cols), BF16),
            pltpu.VMEM((1, cols), F32),
            pltpu.VMEM(exon_bins.shape, jnp.int32),
            pltpu.VMEM(exon_count.shape, jnp.int32),
            pltpu.VMEM((chans, cols), BF16),
            pltpu.VMEM((8, tracks), jnp.int32),
            pltpu.VMEM((n, rows, chans), BF16),
            pltpu.VMEM((n, rank + genes, rows), BF16),
            pltpu.VMEM((2, 1, chans), F32),
            pltpu.VMEM((2, 1, chans), F32),
            pltpu.VMEM((m, 8, 128), jnp.int32),
            pltpu.VMEM((n, owned, cols), jnp.int32),
            pltpu.VMEM((n, owned, cols), jnp.int32),
            pltpu.VMEM((n, rows, cols), F32),
            pltpu.VMEM((nc, m, 2 * owned, cols), F32),
            pltpu.VMEM((nc, m, 2 * owned, cols), F32),
            pltpu.VMEM((nc, 2 * owned, cols), F32),
            pltpu.VMEM((nc, m, 2 * owned, cols), F32),
            pltpu.VMEM((n, 2 * owned, cols), F32),
            pltpu.VMEM((rank + 16, cols), F32),
            pltpu.VMEM((2 * rank, 2 * rows), BF16),
            pltpu.VMEM((CHUNKS, rank // 2, wide), F32),
            pltpu.VMEM((n, rank // 2, wide), F32),
            pltpu.VMEM((m, rank // 2, wide), F32),
            pltpu.VMEM((CHUNKS, rank // 2, wide), F32),
            pltpu.VMEM((m, rank, cols + 128), F32),
            pltpu.VMEM((n, rank, cols + 128), F32),
            dma((11,)),
            dma((2,)),
            dma((2,)),
            dma((m,)),
            dma((m,)),
            dma((2, 2)),
            dma((nc, 3)),
            dma((n, 3)),
            dma((n, 4)),
            dma((n,)),
            dma((n,)),
            dma((n,)),
            dma((n,)),
            dma((nc, m)),
            dma((nc, m)),
            dma((nc, m)),
            dma((nc, m)),
            dma((n,)),
            dma((n,)),
            dma((m,)),
            dma((m,)),
            dma((n,)),
            dma((n,)),
            dma((CHUNKS,)),
            dma((n,)),
            dma((m,)),
            dma((m,)),
            dma((n,)),
            dma((CHUNKS,)),
        ],
        compiler_params=pltpu.CompilerParams(
            collective_id=0, has_side_effects=True, vmem_limit_bytes=56 * 2**20
        ),
    )(
        coarse,
        skip_feats,
        conv_taps,
        norm_gain,
        head_weight,
        adapter_down.T,
        adapter_up,
        head_bias.reshape(1, tracks),
        exon_bins,
        exon_count,
        targets,
    )
    held = (cov, loss, down, up, bias)
    cov, loss, down, up, bias = pl.pallas_call(
        emit,
        in_specs=[vm] * 5,
        out_shape=tuple(jax.ShapeDtypeStruct(a.shape, a.dtype) for a in held),
        out_specs=(hbm,) * 5,
        scratch_shapes=[dma((5,))],
    )(*[pltpu.with_memory_space_constraint(h, pltpu.VMEM) for h in held])
    return cov, loss[0, 0], down.T, up, bias.reshape(tracks)


def solution(mesh):
    placed = (
        P("dp", "seq", None),
        P("dp", "seq", None),
        P(),
        P(),
        P(None, "dp"),
        P(),
        P(),
        P(),
        P("dp", "seq", None),
        P("dp", "seq"),
        P("dp", None, None),
    )
    return jax.shard_map(
        functools.partial(local, mesh.shape["dp"], mesh.shape["seq"]),
        mesh=mesh,
        in_specs=placed,
        out_specs=(P("dp", "seq", None), P(), P(), P(), P()),
        check_vma=False,
    )
```

```python
import functools

import jax
import jax.numpy as jnp
from jax import lax
from jax.experimental import pallas as pl
from jax.experimental.pallas import tpu as pltpu
from jax.sharding import PartitionSpec as P

MESH = pl.DeviceIdType.MESH
F32 = jnp.float32
BF16 = jnp.bfloat16
CHUNKS = 8
EDGE = 16


def mm(a, b):
    return jnp.dot(a, b, preferred_element_type=F32)


def mm_nt(a, b):
    return lax.dot_general(a, b, (((1,), (1,)), ((), ())), preferred_element_type=F32)


def mm_tn(a, b):
    return lax.dot_general(a, b, (((0,), (0,)), ((), ())), preferred_element_type=F32)


def kernel(
    n,
    m,
    scale,
    coarse_h,
    skip_h,
    taps_h,
    gain_h,
    weight,
    down_h,
    up_h,
    bias_h,
    bins_h,
    count_h,
    targets,
    cov_out,
    loss_out,
    down_out,
    up_out,
    bias_out,
    coarse,
    skip,
    taps,
    gain,
    down,
    up,
    bias,
    bins,
    count,
    w_vm,
    tfull,
    hid,
    aux,
    halo,
    edge,
    binbuf,
    tsel,
    tgt,
    tlast,
    tin,
    covl,
    covall,
    sig,
    covp,
    covr,
    covt,
    slp,
    covin,
    acc,
    bkc,
    dn,
    dnr,
    dnz,
    dnf,
    ups,
    upt,
    fin,
    fit,
    sem_loc,
    halo_s,
    halo_r,
    bin_s,
    bin_r,
    hid_s,
    hid_r,
    aux_s,
    aux_r,
    tgt_s,
    tgt_r,
    tl_s,
    tl_r,
    ca_s,
    ca_r,
    cov_s,
    cov_r,
    slp_s,
    slp_r,
    co_s,
    co_r,
    us_s,
    us_r,
    fu_s,
    fu_r,
    ut_s,
    ut_r,
    ft_s,
    ft_r,
    ds_s,
    ds_r,
    dz_s,
    dz_r,
    fd_s,
    fd_r,
):
    d = lax.axis_index("dp")
    s = lax.axis_index("seq")
    nc = n // 2
    relay = nc == 4
    chip = d // 2
    core = d % 2
    sib = chip * 2 + (1 - core)
    rows, chans = skip.shape[1], skip.shape[2]
    cols = weight.shape[1]
    owned = bins.shape[1]
    slots = bins.shape[2]
    rank = up.shape[0]
    genes = owned * m
    inner = rows - 2 * EDGE
    mid = inner // 2
    lines = cols // 128
    wide = chans // (CHUNKS // 2)
    tall = rank // 2

    def pair_of(q):
        found, bit = 0, 1
        while bit < nc:
            found = found + bit * (((chip // bit) % 2 + (q // bit) % 2) % 2)
            bit *= 2
        return found

    def send(src, dst, ss, rs, dd, jj):
        return pltpu.make_async_remote_copy(
            src_ref=src,
            dst_ref=dst,
            send_sem=ss,
            recv_sem=rs,
            device_id=(dd, jj),
            device_id_type=MESH,
        )

    def sent(ref, sem):
        send(ref, ref, sem, sem, sib, s).wait_send()

    def got(ref, sem):
        send(ref, ref, sem, sem, sib, s).wait_recv()

    def dp_peer(k):
        return (d + k) % n

    def seq_peer(k):
        return (s + k) % m

    def column(k):
        return pl.ds(pl.multiple_of(k * cols, 128), cols)

    last = nc - 1
    loads = []
    for src, dst in (
        (skip_h, skip),
        (coarse_h, coarse),
        (taps_h, taps),
        (gain_h, gain),
        (bins_h, bins),
        (count_h, count),
        (down_h, down),
        (targets.at[0], tfull),
        (up_h.at[:, column(d)], up),
        (bias_h.at[:, column(d)], bias),
        (weight, w_vm),
    ):
        c = pltpu.make_async_copy(src, dst, sem_loc.at[len(loads)])
        c.start()
        loads.append(c)
    barrier = pltpu.get_barrier_semaphore()
    for k in range(1, m):
        pl.semaphore_signal(barrier, inc=1, device_id=(d, seq_peer(k)), device_id_type=MESH)
    for k in range(1, n):
        pl.semaphore_signal(barrier, inc=1, device_id=(dp_peer(k), s), device_id_type=MESH)

    for c in loads[:2]:
        c.wait()
    rr = lax.broadcasted_iota(jnp.int32, (rows, rows // 2), 0)
    cc = lax.broadcasted_iota(jnp.int32, (rows, rows // 2), 1)
    spread2 = jnp.where(rr // 2 == cc, 1.0, 0.0).astype(BF16)
    merged = (mm(spread2, coarse[0]) + skip[0].astype(F32)).astype(BF16).astype(F32)
    edge[0] = merged[0:1]
    edge[1] = merged[rows - 1 : rows]

    for c in loads[2:6]:
        c.wait()

    def activate(before, at, after):
        mixed = taps[0:1] * before + taps[1:2] * at + taps[2:3] * after
        normed = (
            mixed
            * lax.rsqrt(jnp.mean(mixed * mixed, axis=-1, keepdims=True) + 1e-06)
            * gain[...].reshape(1, chans)
        )
        return jax.nn.gelu(normed).astype(BF16)

    hid[d, 0:inner] = activate(
        pltpu.roll(merged, 1, 0)[EDGE : rows - EDGE],
        merged[EDGE : rows - EDGE],
        pltpu.roll(merged, rows - 1, 0)[EDGE : rows - EDGE],
    )

    cnt = jnp.broadcast_to(count[...].astype(F32), (owned, owned))
    er = lax.broadcasted_iota(jnp.int32, (owned, owned), 0)
    ec = lax.broadcasted_iota(jnp.int32, (owned, owned), 1)
    cnt = jnp.sum(jnp.where(er == ec, cnt, 0.0), axis=1, keepdims=True)
    slot = lax.broadcasted_iota(jnp.int32, (owned, slots), 1).astype(F32)
    binbuf[s] = jnp.full((8, 128), -1, jnp.int32)
    binbuf[s, 0:owned, 0:slots] = jnp.where(slot < cnt, bins[0], -1)

    first, second = pl.ds(0, mid), pl.ds(mid, mid)
    whole, rim = pl.ds(0, inner), pl.ds(inner, 2 * EDGE)
    rims = (pl.ds(inner, EDGE), pl.ds(inner + EDGE, EDGE))

    def block_copy(w, part, sem, to):
        return send(hid.at[w, part], hid.at[w, part], hid_s.at[0], hid_r.at[sem], to, s)

    base = 6 if relay else nc - 1

    def own_copy(k, part, lane):
        if k == 0:
            return block_copy(d, part, base, sib)
        return block_copy(d, part, 3 * (k - 1) + lane if relay else k - 1, 2 * pair_of(k) + core)

    def forward(w, part, q):
        return block_copy(w, part, base + q, sib)

    def arrive(w, part, sem):
        got(hid.at[w, part], hid_r.at[sem])

    def relay_copy(k, lane):
        w = 2 * pair_of(k) + core
        part = ((first, second)[k - 1], rims[k - 1])[lane]
        return block_copy(w, part, 12 if lane else 9 + k, 2 * pair_of(3 - k) + core)

    pl.semaphore_wait(barrier, n + m - 2)

    to_next = send(edge.at[1], halo.at[0], halo_s.at[0], halo_r.at[0], d, (s + 1) % m)
    to_prev = send(edge.at[0], halo.at[1], halo_s.at[1], halo_r.at[1], d, (s + m - 1) % m)

    @pl.when(s < m - 1)
    def _():
        to_next.start()

    @pl.when(s > 0)
    def _():
        to_prev.start()

    if relay:
        own_copy(1, first, 0).start()
        own_copy(2, second, 1).start()
        own_copy(1, second, 1).start()
        own_copy(2, first, 0).start()
    else:
        for k in range(1, nc):
            own_copy(k, whole, 0).start()
    own_copy(0, whole, 0).start()

    for k in range(1, m):
        send(binbuf.at[s], binbuf.at[s], bin_s.at[0], bin_r.at[0], d, seq_peer(k)).start()

    @pl.when(s == 0)
    def _():
        halo[0] = jnp.zeros((1, chans), F32)

    @pl.when(s == m - 1)
    def _():
        halo[1] = jnp.zeros((1, chans), F32)

    for c in loads[6:8]:
        c.wait()
    def owned_rows(x):
        found = x[0:owned]
        for j in range(1, m):
            found = jnp.where(s == j, x[j * owned : (j + 1) * owned], found)
        return found

    want = owned_rows(tfull[...])
    for j in range(n):
        tsel[j] = want[:, j * cols : (j + 1) * cols]
    tgt[d] = tsel[d]
    for c in (0, 1):
        tlast[c] = tfull[:, column(2 * pair_of(last) + c)]
    acc[...] = jnp.zeros(acc.shape, F32)
    dn[...] = jnp.zeros(dn.shape, F32)

    @pl.when(s > 0)
    def _():
        to_next.wait_recv()

    @pl.when(s < m - 1)
    def _():
        to_prev.wait_recv()

    reach = EDGE + 8
    row = lax.broadcasted_iota(jnp.int32, (reach, chans), 0)
    top, low = merged[0:reach], merged[rows - reach :]
    hid[d, inner + EDGE :] = activate(
        jnp.where(row == 0, halo[0], pltpu.roll(top, 1, 0))[0:EDGE],
        top[0:EDGE],
        pltpu.roll(top, reach - 1, 0)[0:EDGE],
    )
    hid[d, inner : inner + EDGE] = activate(
        pltpu.roll(low, 1, 0)[8:],
        low[8:],
        jnp.where(row == reach - 1, halo[1], pltpu.roll(low, reach - 1, 0))[8:],
    )
    for k in range(1, 3 if relay else nc):
        own_copy(k, rim, 2).start()
    own_copy(0, rim, 2).start()

    aux[d, 0:rank] = mm_nt(down[...], hid[d]).astype(BF16)

    got(binbuf.at[pl.ds(0, m - 1)], bin_r.at[0])
    listed = jnp.concatenate([binbuf[j][0:owned] for j in range(m)], axis=0)
    here = s * rows + (lax.broadcasted_iota(jnp.int32, (genes, rows), 1) + EDGE) % rows
    member = jnp.zeros((genes, rows), F32)
    for j in range(slots):
        member += jnp.where(listed[:, j : j + 1] == here, 1.0, 0.0)
    aux[d, rank : rank + genes] = member.astype(BF16)

    def aux_copy(w, to, sem):
        return send(aux.at[w], aux.at[w], aux_s.at[0], aux_r.at[sem], to, s)

    def tgt_copy(src, w, to, sem):
        return send(src, tgt.at[w], tgt_s.at[0], tgt_r.at[sem], to, s)

    aux_copy(d, sib, 1).start()
    for k in range(1, nc):
        aux_copy(d, 2 * pair_of(k) + core, 0).start()
    for k in range(1, n):
        j = dp_peer(k)
        tgt_copy(tsel.at[j], d, j, 0).start()

    for c in loads[8:]:
        c.wait()

    def window(p, u):
        return 2 * p + (core if u == 0 else 1 - core)

    def cov_copy(p, j):
        return send(covp.at[p, j], covr.at[p, s], cov_s.at[0], cov_r.at[p], d, j)

    def slp_copy(p, k):
        return send(slp.at[p, s], slp.at[p, s], slp_s.at[0], slp_r.at[p], d, seq_peer(k))

    def out_copy(p, w):
        return send(covt.at[p], covin.at[d], co_s.at[0], co_r.at[0], w, s)

    def tlast_copy(c):
        return send(tlast.at[c], tin.at[core], tl_s.at[0], tl_r.at[0], 2 * pair_of(last) + c, s)

    def all_copy(u, k):
        return send(covl.at[u], covall.at[s, u], ca_s.at[0], ca_r.at[0], d, seq_peer(k))

    def head(w):
        out = mm(hid[w], w_vm[...])
        out += mm_tn(aux[w, 0:rank], up[...])
        out += bias[...]
        e = jnp.exp(-jnp.abs(out))
        r = 1.0 / (1.0 + e)
        sig[w] = jnp.where(out >= 0, r, e * r)
        predicted = jnp.maximum(out, 0.0) + jnp.log1p(e)
        high = predicted.astype(BF16)
        low = (predicted - high.astype(F32)).astype(BF16)
        mem = aux[w, rank : rank + genes]
        return mm(mem, high) + mm(mem, low)

    def head_stage(q):
        p = pair_of(q)
        parts = []
        for u in range(2):
            w = window(p, u)

            if u == 0:

                if relay:

                    @pl.when(q == 1)
                    def _():
                        near = [2 * pair_of(k) + core for k in (1, 2)]
                        arrive(near[0], second, 1)
                        forward(near[0], whole, 1).start()
                        arrive(near[1], first, 3)
                        forward(near[1], whole, 2).start()
                        for k in (1, 2):
                            arrive(near[k - 1], rim, 3 * k - 1)
                            relay_copy(k, 1).start()
                            forward(near[k - 1], rim, k).start()

                else:

                    @pl.when(q > 0)
                    def _():
                        got(hid.at[w], hid_r.at[q - 1])
                        send(hid.at[w], hid.at[w], hid_s.at[0], hid_r.at[base + q], sib, s).start()

                @pl.when(q == 1)
                def _():
                    got(aux.at[pl.ds(0, nc - 1)], aux_r.at[0])
                    for k in range(1, nc):
                        aux_copy(2 * pair_of(k) + core, sib, 2).start()
                    for c in (0, 1):
                        tlast_copy(c).start()

            else:
                if relay:

                    @pl.when(q == 0)
                    def _():
                        arrive(2 * pair_of(1) + core, first, 0)
                        relay_copy(1, 0).start()
                        arrive(2 * pair_of(2) + core, second, 4)
                        relay_copy(2, 0).start()

                got(hid.at[w], hid_r.at[base + q])

                @pl.when(q == 0)
                def _():
                    got(aux.at[0], aux_r.at[1])

                @pl.when(q == 1)
                def _():
                    got(aux.at[pl.ds(0, nc - 1)], aux_r.at[2])

            parts.append(head(w))
        for j in range(m):
            covp[p, j] = jnp.concatenate(
                [part[j * owned : (j + 1) * owned] for part in parts], axis=0
            )
        covr[p, s] = covp[p, s]
        for k in range(1, m):
            cov_copy(p, seq_peer(k)).start()

    def head_last():
        p = pair_of(last)
        for u in range(2):
            w = window(p, u)
            if u == 0:
                if relay:
                    arrive(w, first, 10)
                    forward(w, first, 3).start()
                    arrive(w, second, 11)
                    forward(w, second, 3).start()
                    arrive(w, rim, 12)
                    forward(w, rim, 3).start()
                else:
                    got(hid.at[w], hid_r.at[last - 1])
                    send(hid.at[w], hid.at[w], hid_s.at[0], hid_r.at[base + last], sib, s).start()
            else:
                if last >= 2:
                    slope_stage(last - 2)
                got(hid.at[w], hid_r.at[base + last])
            part = head(w)
            covl[u] = part
            covall[s, u] = part
            for k in range(1, m):
                all_copy(u, k).start()

    def slope_last():
        p = pair_of(last)
        got(tin, tl_r.at[0])
        got(covall.at[pl.ds(0, m - 1)], ca_r.at[0])
        slopes, totals, wants = [], [], []
        for u in range(2):
            total = covall[0, u]
            for j in range(1, m):
                total += covall[j, u]
            want = tin[core if u == 0 else 1 - core].astype(F32)
            slopes.append(scale * (1.0 - want / (1.0 + total)))
            totals.append(owned_rows(total))
            wants.append(owned_rows(want))
        total = jnp.concatenate(totals, axis=0)
        covt[p] = total
        for u in range(2):
            out_copy(p, window(p, u)).start()
        acc[rank + 8 :] += total - jnp.concatenate(wants, axis=0) * jnp.log1p(total)
        return slopes

    def slope_stage(q):
        p = pair_of(q)

        @pl.when(q == 0)
        def _():
            got(tgt.at[pl.ds(0, n - 1)], tgt_r.at[0])

        wants = [tgt[window(p, u)].astype(F32) for u in range(2)]
        want = jnp.concatenate(wants, axis=0)
        got(covr.at[p, pl.ds(0, m - 1)], cov_r.at[p])
        total = covr[p, 0]
        for j in range(1, m):
            total += covr[p, j]
        slp[p, s] = scale * (1.0 - want / (1.0 + total))
        for k in range(1, m):
            slp_copy(p, k).start()
        covt[p] = total
        acc[rank + 8 :] += total - want * jnp.log1p(total)

        @pl.when(q > 0)
        def _():
            out_copy(p, window(p, 0)).start()

        out_copy(p, window(p, 1)).start()

    def grad_rows(p, slopes_of):
        halves = []
        for u in range(2):
            w = window(p, u)
            slopes = slopes_of[u]
            s0 = slopes.astype(BF16)
            left = slopes - s0.astype(F32)
            s1 = left.astype(BF16)
            s2 = (left - s1.astype(F32)).astype(BF16)
            mem = aux[w, rank : rank + genes]
            spread = mm_tn(
                jnp.concatenate([mem, mem, mem], axis=0), jnp.concatenate([s0, s1, s2], axis=0)
            )
            grad = spread * sig[w]
            half = grad.astype(BF16)
            acc[0:rank] += mm(aux[w, 0:rank], half)
            acc[rank : rank + 8] += jnp.sum(grad.reshape(rows // 8, 8, cols), axis=0)
            halves.append(half)
        return halves

    def grad_back(p, halves):
        for u in range(2):
            back = mm_nt(up[...], halves[u])
            high = back.astype(BF16)
            low = (back - high.astype(F32)).astype(BF16)
            side = core if u == 0 else 1 - core
            bkc[:, pl.ds(pl.multiple_of(side * rows, 128), rows)] = jnp.concatenate(
                [high, low], axis=0
            )
        both = mm(bkc[...], hid[pl.ds(2 * p, 2)].reshape(2 * rows, chans))
        both = both[0:rank] + both[rank:]
        for k in range(CHUNKS):
            y, x = (k % 2) * tall, (k // 2) * wide
            dn[k] += both[y : y + tall, x : x + wide]

    def slopes_in(q):
        p = pair_of(q)
        got(slp.at[p, pl.ds(0, m - 1)], slp_r.at[p])
        return [
            jnp.concatenate([slp[p, j][u * owned : (u + 1) * owned] for j in range(m)], axis=0)
            for u in range(2)
        ]

    def grad_stage(q):
        p = pair_of(q)
        grad_back(p, grad_rows(p, slopes_in(q)))

    def step(q, carry):
        head_stage(q)

        @pl.when(q >= 2)
        def _():
            slope_stage(q - 2)

        if last > 4:

            @pl.when(q >= 4)
            def _():
                grad_stage(q - 4)

        return carry

    lax.fori_loop(0, last, step, 0)
    head_last()
    slope_stage(last - 1)
    for q in range(max(0, last - 4), last - 1):
        grad_stage(q)
    late = [(pair_of(last), grad_rows(pair_of(last), slope_last()))]
    late.append((pair_of(last - 1), grad_rows(pair_of(last - 1), slopes_in(last - 1))))

    for p, halves in late:
        grad_back(p, halves)

    def part_copy(j):
        return send(dn.at[j], dnr.at[d], ds_s.at[0], ds_r.at[0], j, s)

    def if_owner(f):
        if n > CHUNKS:
            pl.when(d < CHUNKS)(f)
        else:
            f()

    def if_other(j, f):
        pl.when(d != j)(f)

    for j in range(CHUNKS):
        if_other(j, lambda: part_copy(j).start())

    ups[s, :, 0:cols] = acc[0:tall]
    bias_sum = jnp.sum(acc[rank : rank + 8], axis=0, keepdims=True)
    loss_sum = scale * jnp.sum(acc[rank + 8 :], axis=0, keepdims=True)
    small = [bias_sum[:, i * 128 : (i + 1) * 128] for i in range(lines)]
    small += [loss_sum[:, i * 128 : (i + 1) * 128] for i in range(lines)]
    if tall > 2 * lines:
        small.append(jnp.zeros((tall - 2 * lines, 128), F32))
    ups[s, :, cols:] = jnp.concatenate(small, axis=0)
    upt[s] = acc[tall:rank]
    for k in range(1, m):
        send(ups.at[s], ups.at[s], us_s.at[0], us_r.at[0], d, seq_peer(k)).start()
    for k in range(1, m):
        send(upt.at[s], upt.at[s], ut_s.at[0], ut_r.at[0], d, seq_peer(k)).start()
    covin[d] = covt[chip]
    got(covin.at[pl.ds(0, n - 1)], co_r.at[0])
    for j in range(n):
        both = covin[j]
        cov_out[0, :, j * cols : (j + 1) * cols] = jnp.where(
            core == j % 2, both[0:owned], both[owned : 2 * owned]
        )

    @pl.when(s < m - 1)
    def _():
        to_next.wait_send()

    @pl.when(s > 0)
    def _():
        to_prev.wait_send()

    sent(binbuf.at[pl.ds(0, m - 1)], bin_s.at[0])
    sent(hid.at[pl.ds(0, n - 1)], hid_s.at[0])
    sent(aux.at[pl.ds(0, n - 1)], aux_s.at[0])
    sent(tgt.at[pl.ds(0, n - 1)], tgt_s.at[0])
    sent(covp.at[pl.ds(0, last), pl.ds(0, m - 1)], cov_s.at[0])
    sent(slp.at[pl.ds(0, last), pl.ds(0, m - 1)], slp_s.at[0])
    sent(tlast, tl_s.at[0])
    sent(covall.at[pl.ds(0, m - 1)], ca_s.at[0])
    sent(covin.at[pl.ds(0, n - 1)], co_s.at[0])

    def gathered_z(k):
        j = seq_peer(k)
        return send(dnz.at[s], dnz.at[s], dz_s.at[0], dz_r.at[0], d, j)

    def spread_part(k):
        return send(dnf.at[d], dnf.at[d], fd_s.at[0], fd_r.at[0], dp_peer(k), s)

    def sum_plane():
        dnr[d] = dn[d]
        got(dnr.at[pl.ds(0, n - 1)], ds_r.at[0])
        total = dnr[0]
        for j in range(1, n):
            total += dnr[j]
        dnz[s] = total
        for k in range(1, m):
            gathered_z(k).start()

    if_owner(sum_plane)

    for held, full, zr, ps, pr in ((ups, fin, us_r, fu_s, fu_r), (upt, fit, ut_r, ft_s, ft_r)):
        got(held.at[pl.ds(0, m - 1)], zr.at[0])
        total = held[0]
        for j in range(1, m):
            total += held[j]
        full[d] = total
        for k in range(1, n):
            send(full.at[d], full.at[d], ps.at[0], pr.at[0], dp_peer(k), s).start()

    def sum_seq():
        got(dnz.at[pl.ds(0, m - 1)], dz_r.at[0])
        total = dnz[0]
        for j in range(1, m):
            total += dnz[j]
        dnf[d] = total
        for k in range(1, n):
            spread_part(k).start()

    if_owner(sum_seq)

    def if_sender(f, g):
        if n > CHUNKS:
            pl.when(d < CHUNKS)(f)
            pl.when(d >= CHUNKS)(g)
        else:
            f()

    sent(ups.at[pl.ds(0, m - 1)], us_s.at[0])
    sent(upt.at[pl.ds(0, m - 1)], ut_s.at[0])
    if_sender(
        lambda: sent(dn.at[pl.ds(0, CHUNKS - 1)], ds_s.at[0]),
        lambda: sent(dn, ds_s.at[0]),
    )
    if_owner(lambda: sent(dnz.at[pl.ds(0, m - 1)], dz_s.at[0]))

    got(fin.at[pl.ds(0, n - 1)], fu_r.at[0])
    loss = jnp.zeros((lines, 128), F32)
    for j in range(n):
        up_out[0:tall, j * cols : (j + 1) * cols] = fin[j, :, 0:cols]
        for i in range(lines):
            x = j * cols + i * 128
            bias_out[:, x : x + 128] = fin[j, i : i + 1, cols:]
        loss += fin[j, lines : 2 * lines, cols:]
    got(fit.at[pl.ds(0, n - 1)], ft_r.at[0])
    for j in range(n):
        up_out[tall:rank, j * cols : (j + 1) * cols] = fit[j]
    loss_out[...] = jnp.sum(jnp.sum(loss, axis=0, keepdims=True), axis=1, keepdims=True)

    if_sender(
        lambda: got(dnf.at[pl.ds(0, CHUNKS - 1)], fd_r.at[0]),
        lambda: got(dnf, fd_r.at[0]),
    )
    for j in range(CHUNKS):
        y, x = (j % 2) * tall, (j // 2) * wide
        down_out[y : y + tall, x : x + wide] = dnf[j]

    sent(fin.at[pl.ds(0, n - 1)], fu_s.at[0])
    sent(fit.at[pl.ds(0, n - 1)], ft_s.at[0])
    if_owner(lambda: sent(dnr.at[pl.ds(0, n - 1)], fd_s.at[0]))


def emit(*refs):
    sems = refs[-1]
    k = (len(refs) - 1) // 2
    copies = [
        pltpu.make_async_copy(refs[i], refs[k + i], sems.at[i]) for i in range(k)
    ]
    for c in copies:
        c.start()
    for c in copies:
        c.wait()


def local(
    n,
    m,
    coarse,
    skip_feats,
    conv_taps,
    norm_gain,
    head_weight,
    adapter_down,
    adapter_up,
    head_bias,
    exon_bins,
    exon_count,
    targets,
):
    rows, chans = skip_feats.shape[1:]
    cols = head_weight.shape[1]
    tracks = adapter_up.shape[1]
    rank = adapter_up.shape[0]
    owned = exon_bins.shape[1]
    genes = owned * m
    nc = n // 2
    wide = chans // (CHUNKS // 2)
    scale = 1.0 / (n * genes)
    vm = pl.BlockSpec(memory_space=pltpu.VMEM)
    hbm = pl.BlockSpec(memory_space=pltpu.HBM)
    dma = pltpu.SemaphoreType.DMA
    cov, loss, down, up, bias = pl.pallas_call(
        functools.partial(kernel, n, m, scale),
        out_shape=(
            pltpu.VMEM((1, owned, tracks), F32),
            pltpu.VMEM((1, 1), F32),
            pltpu.VMEM((rank, chans), F32),
            pltpu.VMEM((rank, tracks), F32),
            pltpu.VMEM((1, tracks), F32),
        ),
        in_specs=[hbm] * 11,
        out_specs=(vm,) * 5,
        scratch_shapes=[
            pltpu.VMEM((1, rows // 2, chans), BF16),
            pltpu.VMEM((1, rows, chans), BF16),
            pltpu.VMEM(conv_taps.shape, F32),
            pltpu.VMEM((chans,), F32),
            pltpu.VMEM((rank, chans), BF16),
            pltpu.VMEM((rank, cols), BF16),
            pltpu.VMEM((1, cols), F32),
            pltpu.VMEM(exon_bins.shape, jnp.int32),
            pltpu.VMEM(exon_count.shape, jnp.int32),
            pltpu.VMEM((chans, cols), BF16),
            pltpu.VMEM((genes, tracks), jnp.int32),
            pltpu.VMEM((n, rows, chans), BF16),
            pltpu.VMEM((n, rank + genes, rows), BF16),
            pltpu.VMEM((2, 1, chans), F32),
            pltpu.VMEM((2, 1, chans), F32),
            pltpu.VMEM((m, 8, 128), jnp.int32),
            pltpu.VMEM((n, owned, cols), jnp.int32),
            pltpu.VMEM((n, owned, cols), jnp.int32),
            pltpu.VMEM((2, genes, cols), jnp.int32),
            pltpu.VMEM((2, genes, cols), jnp.int32),
            pltpu.VMEM((2, genes, cols), F32),
            pltpu.VMEM((m, 2, genes, cols), F32),
            pltpu.VMEM((n, rows, cols), F32),
            pltpu.VMEM((nc, m, 2 * owned, cols), F32),
            pltpu.VMEM((nc, m, 2 * owned, cols), F32),
            pltpu.VMEM((nc, 2 * owned, cols), F32),
            pltpu.VMEM((nc, m, 2 * owned, cols), F32),
            pltpu.VMEM((n, 2 * owned, cols), F32),
            pltpu.VMEM((rank + 16, cols), F32),
            pltpu.VMEM((2 * rank, 2 * rows), BF16),
            pltpu.VMEM((CHUNKS, rank // 2, wide), F32),
            pltpu.VMEM((n, rank // 2, wide), F32),
            pltpu.VMEM((m, rank // 2, wide), F32),
            pltpu.VMEM((CHUNKS, rank // 2, wide), F32),
            pltpu.VMEM((m, rank // 2, cols + 128), F32),
            pltpu.VMEM((m, rank // 2, cols), F32),
            pltpu.VMEM((n, rank // 2, cols + 128), F32),
            pltpu.VMEM((n, rank // 2, cols), F32),
            dma((11,)),
            dma((2,)),
            dma((2,)),
            dma((1,)),
            dma((1,)),
            dma((1,)),
            dma((13 if nc == 4 else n - 1,)),
            dma((1,)),
            dma((3,)),
            dma((1,)),
            dma((1,)),
            dma((1,)),
            dma((1,)),
            dma((1,)),
            dma((1,)),
            dma((1,)),
            dma((nc,)),
            dma((1,)),
            dma((nc,)),
        ]
        + [dma((1,))] * 16,
        compiler_params=pltpu.CompilerParams(
            collective_id=0, has_side_effects=True, vmem_limit_bytes=56 * 2**20
        ),
    )(
        coarse,
        skip_feats,
        conv_taps,
        norm_gain,
        head_weight,
        adapter_down.T,
        adapter_up,
        head_bias.reshape(1, tracks),
        exon_bins,
        exon_count,
        targets,
    )
    held = (cov, loss, down, up, bias)
    cov, loss, down, up, bias = pl.pallas_call(
        emit,
        in_specs=[vm] * 5,
        out_shape=tuple(jax.ShapeDtypeStruct(a.shape, a.dtype) for a in held),
        out_specs=(hbm,) * 5,
        scratch_shapes=[dma((5,))],
    )(*[pltpu.with_memory_space_constraint(h, pltpu.VMEM) for h in held])
    return cov, loss[0, 0], down.T, up, bias.reshape(tracks)


def solution(mesh):
    placed = (
        P("dp", "seq", None),
        P("dp", "seq", None),
        P(),
        P(),
        P(None, "dp"),
        P(),
        P(),
        P(),
        P("dp", "seq", None),
        P("dp", "seq"),
        P("dp", None, None),
    )
    return jax.shard_map(
        functools.partial(local, mesh.shape["dp"], mesh.shape["seq"]),
        mesh=mesh,
        in_specs=placed,
        out_specs=(P("dp", "seq", None), P(), P(), P(), P()),
        check_vma=False,
    )
```

```python
import functools

import jax
import jax.numpy as jnp
from jax import lax
from jax.experimental import pallas as pl
from jax.experimental.pallas import tpu as pltpu
from jax.sharding import PartitionSpec as P

MESH = pl.DeviceIdType.MESH
F32 = jnp.float32
BF16 = jnp.bfloat16
CHUNKS = 8
EDGE = 16


def mm(a, b):
    return jnp.dot(a, b, preferred_element_type=F32)


def mm_nt(a, b):
    return lax.dot_general(a, b, (((1,), (1,)), ((), ())), preferred_element_type=F32)


def mm_tn(a, b):
    return lax.dot_general(a, b, (((0,), (0,)), ((), ())), preferred_element_type=F32)


def kernel(
    n,
    m,
    scale,
    coarse_h,
    skip_h,
    taps_h,
    gain_h,
    weight,
    down_h,
    up_h,
    bias_h,
    bins_h,
    count_h,
    targets,
    cov_out,
    loss_out,
    down_out,
    up_out,
    bias_out,
    coarse,
    skip,
    taps,
    gain,
    down,
    up,
    bias,
    bins,
    count,
    w_vm,
    tfull,
    hid,
    aux,
    halo,
    edge,
    binbuf,
    tsel,
    tgt,
    tlast,
    tin,
    covl,
    covall,
    sig,
    covp,
    covr,
    covt,
    slp,
    covin,
    acc,
    bkc,
    dn,
    dnr,
    dnz,
    dnf,
    ups,
    upt,
    fin,
    fit,
    sem_loc,
    halo_s,
    halo_r,
    bin_s,
    bin_r,
    hid_s,
    hid_r,
    aux_s,
    aux_r,
    tgt_s,
    tgt_r,
    tl_s,
    tl_r,
    ca_s,
    ca_r,
    cov_s,
    cov_r,
    slp_s,
    slp_r,
    co_s,
    co_r,
    us_s,
    us_r,
    fu_s,
    fu_r,
    ut_s,
    ut_r,
    ft_s,
    ft_r,
    ds_s,
    ds_r,
    dz_s,
    dz_r,
    fd_s,
    fd_r,
):
    d = lax.axis_index("dp")
    s = lax.axis_index("seq")
    nc = n // 2
    relay = nc == 4
    chip = d // 2
    core = d % 2
    sib = chip * 2 + (1 - core)
    rows, chans = skip.shape[1], skip.shape[2]
    cols = weight.shape[1]
    owned = bins.shape[1]
    slots = bins.shape[2]
    rank = up.shape[0]
    genes = owned * m
    inner = rows - 2 * EDGE
    mid = inner // 2
    lines = cols // 128
    wide = chans // (CHUNKS // 2)
    tall = rank // 2

    def pair_of(q):
        found, bit = 0, 1
        while bit < nc:
            found = found + bit * (((chip // bit) % 2 + (q // bit) % 2) % 2)
            bit *= 2
        return found

    def send(src, dst, ss, rs, dd, jj):
        return pltpu.make_async_remote_copy(
            src_ref=src,
            dst_ref=dst,
            send_sem=ss,
            recv_sem=rs,
            device_id=(dd, jj),
            device_id_type=MESH,
        )

    def sent(ref, sem):
        send(ref, ref, sem, sem, sib, s).wait_send()

    def got(ref, sem):
        send(ref, ref, sem, sem, sib, s).wait_recv()

    def dp_peer(k):
        return (d + k) % n

    def seq_peer(k):
        return (s + k) % m

    def column(k):
        return pl.ds(pl.multiple_of(k * cols, 128), cols)

    last = nc - 1
    loads = []
    for src, dst in (
        (skip_h, skip),
        (coarse_h, coarse),
        (taps_h, taps),
        (gain_h, gain),
        (bins_h, bins),
        (count_h, count),
        (down_h, down),
        (targets.at[0], tfull),
        (up_h.at[:, column(d)], up),
        (bias_h.at[:, column(d)], bias),
        (weight, w_vm),
    ):
        c = pltpu.make_async_copy(src, dst, sem_loc.at[len(loads)])
        c.start()
        loads.append(c)
    barrier = pltpu.get_barrier_semaphore()
    for k in range(1, m):
        pl.semaphore_signal(barrier, inc=1, device_id=(d, seq_peer(k)), device_id_type=MESH)
    for k in range(1, n):
        pl.semaphore_signal(barrier, inc=1, device_id=(dp_peer(k), s), device_id_type=MESH)

    for c in loads[:2]:
        c.wait()
    rr = lax.broadcasted_iota(jnp.int32, (rows, rows // 2), 0)
    cc = lax.broadcasted_iota(jnp.int32, (rows, rows // 2), 1)
    spread2 = jnp.where(rr // 2 == cc, 1.0, 0.0).astype(BF16)
    merged = (mm(spread2, coarse[0]) + skip[0].astype(F32)).astype(BF16).astype(F32)
    edge[0] = merged[0:1]
    edge[1] = merged[rows - 1 : rows]

    for c in loads[2:6]:
        c.wait()

    def activate(before, at, after):
        mixed = taps[0:1] * before + taps[1:2] * at + taps[2:3] * after
        normed = (
            mixed
            * lax.rsqrt(jnp.mean(mixed * mixed, axis=-1, keepdims=True) + 1e-06)
            * gain[...].reshape(1, chans)
        )
        return jax.nn.gelu(normed).astype(BF16)

    hid[d, 0:inner] = activate(
        pltpu.roll(merged, 1, 0)[EDGE : rows - EDGE],
        merged[EDGE : rows - EDGE],
        pltpu.roll(merged, rows - 1, 0)[EDGE : rows - EDGE],
    )

    cnt = jnp.broadcast_to(count[...].astype(F32), (owned, owned))
    er = lax.broadcasted_iota(jnp.int32, (owned, owned), 0)
    ec = lax.broadcasted_iota(jnp.int32, (owned, owned), 1)
    cnt = jnp.sum(jnp.where(er == ec, cnt, 0.0), axis=1, keepdims=True)
    slot = lax.broadcasted_iota(jnp.int32, (owned, slots), 1).astype(F32)
    binbuf[s] = jnp.full((8, 128), -1, jnp.int32)
    binbuf[s, 0:owned, 0:slots] = jnp.where(slot < cnt, bins[0], -1)

    first, second = pl.ds(0, mid), pl.ds(mid, mid)
    whole, rim = pl.ds(0, inner), pl.ds(inner, 2 * EDGE)
    rims = (pl.ds(inner, EDGE), pl.ds(inner + EDGE, EDGE))

    def block_copy(w, part, sem, to):
        return send(hid.at[w, part], hid.at[w, part], hid_s.at[0], hid_r.at[sem], to, s)

    base = 6 if relay else nc - 1

    def own_copy(k, part, lane):
        if k == 0:
            return block_copy(d, part, base, sib)
        return block_copy(d, part, 3 * (k - 1) + lane if relay else k - 1, 2 * pair_of(k) + core)

    def forward(w, part, q):
        return block_copy(w, part, base + q, sib)

    def arrive(w, part, sem):
        got(hid.at[w, part], hid_r.at[sem])

    def relay_copy(k, lane):
        w = 2 * pair_of(k) + core
        part = ((first, second)[k - 1], rims[k - 1])[lane]
        return block_copy(w, part, 12 if lane else 9 + k, 2 * pair_of(3 - k) + core)

    pl.semaphore_wait(barrier, n + m - 2)

    to_next = send(edge.at[1], halo.at[0], halo_s.at[0], halo_r.at[0], d, (s + 1) % m)
    to_prev = send(edge.at[0], halo.at[1], halo_s.at[1], halo_r.at[1], d, (s + m - 1) % m)

    @pl.when(s < m - 1)
    def _():
        to_next.start()

    @pl.when(s > 0)
    def _():
        to_prev.start()

    if relay:
        own_copy(1, first, 0).start()
        own_copy(2, second, 1).start()
        own_copy(1, second, 1).start()
        own_copy(2, first, 0).start()
    else:
        for k in range(1, nc):
            own_copy(k, whole, 0).start()
    own_copy(0, whole, 0).start()

    for k in range(1, m):
        send(binbuf.at[s], binbuf.at[s], bin_s.at[0], bin_r.at[0], d, seq_peer(k)).start()

    @pl.when(s == 0)
    def _():
        halo[0] = jnp.zeros((1, chans), F32)

    @pl.when(s == m - 1)
    def _():
        halo[1] = jnp.zeros((1, chans), F32)

    for c in loads[6:8]:
        c.wait()
    def owned_rows(x):
        found = x[0:owned]
        for j in range(1, m):
            found = jnp.where(s == j, x[j * owned : (j + 1) * owned], found)
        return found

    want = owned_rows(tfull[...])
    for j in range(n):
        tsel[j] = want[:, j * cols : (j + 1) * cols]
    tgt[d] = tsel[d]
    for c in (0, 1):
        tlast[c] = tfull[:, column(2 * pair_of(last) + c)]
    acc[...] = jnp.zeros(acc.shape, F32)
    dn[...] = jnp.zeros(dn.shape, F32)

    @pl.when(s > 0)
    def _():
        to_next.wait_recv()

    @pl.when(s < m - 1)
    def _():
        to_prev.wait_recv()

    reach = EDGE + 8
    row = lax.broadcasted_iota(jnp.int32, (reach, chans), 0)
    top, low = merged[0:reach], merged[rows - reach :]
    hid[d, inner + EDGE :] = activate(
        jnp.where(row == 0, halo[0], pltpu.roll(top, 1, 0))[0:EDGE],
        top[0:EDGE],
        pltpu.roll(top, reach - 1, 0)[0:EDGE],
    )
    hid[d, inner : inner + EDGE] = activate(
        pltpu.roll(low, 1, 0)[8:],
        low[8:],
        jnp.where(row == reach - 1, halo[1], pltpu.roll(low, reach - 1, 0))[8:],
    )
    for k in range(1, 3 if relay else nc):
        own_copy(k, rim, 2).start()
    own_copy(0, rim, 2).start()

    aux[d, 0:rank] = mm_nt(down[...], hid[d]).astype(BF16)

    got(binbuf.at[pl.ds(0, m - 1)], bin_r.at[0])
    listed = jnp.concatenate([binbuf[j][0:owned] for j in range(m)], axis=0)
    here = s * rows + (lax.broadcasted_iota(jnp.int32, (genes, rows), 1) + EDGE) % rows
    member = jnp.zeros((genes, rows), F32)
    for j in range(slots):
        member += jnp.where(listed[:, j : j + 1] == here, 1.0, 0.0)
    aux[d, rank : rank + genes] = member.astype(BF16)

    def aux_copy(w, to, sem):
        return send(aux.at[w], aux.at[w], aux_s.at[0], aux_r.at[sem], to, s)

    def tgt_copy(src, w, to, sem):
        return send(src, tgt.at[w], tgt_s.at[0], tgt_r.at[sem], to, s)

    aux_copy(d, sib, 1).start()
    for k in range(1, nc):
        aux_copy(d, 2 * pair_of(k) + core, 0).start()
    for k in range(1, n):
        j = dp_peer(k)
        tgt_copy(tsel.at[j], d, j, 0).start()

    for c in loads[8:]:
        c.wait()

    def window(p, u):
        return 2 * p + (core if u == 0 else 1 - core)

    def cov_copy(p, j):
        return send(covp.at[p, j], covr.at[p, s], cov_s.at[0], cov_r.at[p], d, j)

    def slp_copy(p, k):
        return send(slp.at[p, s], slp.at[p, s], slp_s.at[0], slp_r.at[p], d, seq_peer(k))

    def out_copy(p, w):
        return send(covt.at[p], covin.at[d], co_s.at[0], co_r.at[0], w, s)

    def tlast_copy(c):
        return send(tlast.at[c], tin.at[core], tl_s.at[0], tl_r.at[0], 2 * pair_of(last) + c, s)

    def all_copy(u, k):
        return send(covl.at[u], covall.at[s, u], ca_s.at[0], ca_r.at[0], d, seq_peer(k))

    def head(w):
        out = mm(hid[w], w_vm[...])
        out += mm_tn(aux[w, 0:rank], up[...])
        out += bias[...]
        e = jnp.exp(-jnp.abs(out))
        r = 1.0 / (1.0 + e)
        sig[w] = jnp.where(out >= 0, r, e * r)
        predicted = jnp.maximum(out, 0.0) + jnp.log1p(e)
        high = predicted.astype(BF16)
        low = (predicted - high.astype(F32)).astype(BF16)
        mem = aux[w, rank : rank + genes]
        return mm(mem, high) + mm(mem, low)

    def head_stage(q):
        p = pair_of(q)
        parts = []
        for u in range(2):
            w = window(p, u)

            if u == 0:

                if relay:

                    @pl.when(q == 1)
                    def _():
                        near = [2 * pair_of(k) + core for k in (1, 2)]
                        arrive(near[0], second, 1)
                        forward(near[0], whole, 1).start()
                        arrive(near[1], first, 3)
                        forward(near[1], whole, 2).start()
                        for k in (1, 2):
                            arrive(near[k - 1], rim, 3 * k - 1)
                            relay_copy(k, 1).start()
                            forward(near[k - 1], rim, k).start()

                else:

                    @pl.when(q > 0)
                    def _():
                        got(hid.at[w], hid_r.at[q - 1])
                        send(hid.at[w], hid.at[w], hid_s.at[0], hid_r.at[base + q], sib, s).start()

                @pl.when(q == 1)
                def _():
                    got(aux.at[pl.ds(0, nc - 1)], aux_r.at[0])
                    for k in range(1, nc):
                        aux_copy(2 * pair_of(k) + core, sib, 2).start()
                    for c in (0, 1):
                        tlast_copy(c).start()

            else:
                if relay:

                    @pl.when(q == 0)
                    def _():
                        arrive(2 * pair_of(1) + core, first, 0)
                        relay_copy(1, 0).start()
                        arrive(2 * pair_of(2) + core, second, 4)
                        relay_copy(2, 0).start()

                got(hid.at[w], hid_r.at[base + q])

                @pl.when(q == 0)
                def _():
                    got(aux.at[0], aux_r.at[1])

                @pl.when(q == 1)
                def _():
                    got(aux.at[pl.ds(0, nc - 1)], aux_r.at[2])

            parts.append(head(w))
        for j in range(m):
            covp[p, j] = jnp.concatenate(
                [part[j * owned : (j + 1) * owned] for part in parts], axis=0
            )
        covr[p, s] = covp[p, s]
        for k in range(1, m):
            cov_copy(p, seq_peer(k)).start()

    def head_last():
        p = pair_of(last)
        for u in range(2):
            w = window(p, u)
            if u == 0:
                if relay:
                    arrive(w, first, 10)
                    forward(w, first, 3).start()
                    arrive(w, second, 11)
                    forward(w, second, 3).start()
                    arrive(w, rim, 12)
                    forward(w, rim, 3).start()
                else:
                    got(hid.at[w], hid_r.at[last - 1])
                    send(hid.at[w], hid.at[w], hid_s.at[0], hid_r.at[base + last], sib, s).start()
            else:
                if last >= 2:
                    slope_stage(last - 2)
                got(hid.at[w], hid_r.at[base + last])
            part = head(w)
            covl[u] = part
            covall[s, u] = part
            for k in range(1, m):
                all_copy(u, k).start()

    def slope_last():
        p = pair_of(last)
        got(tin, tl_r.at[0])
        got(covall.at[pl.ds(0, m - 1)], ca_r.at[0])
        slopes, totals, wants = [], [], []
        for u in range(2):
            total = covall[0, u]
            for j in range(1, m):
                total += covall[j, u]
            want = tin[core if u == 0 else 1 - core].astype(F32)
            slopes.append(scale * (1.0 - want / (1.0 + total)))
            totals.append(owned_rows(total))
            wants.append(owned_rows(want))
        total = jnp.concatenate(totals, axis=0)
        covt[p] = total
        for u in range(2):
            out_copy(p, window(p, u)).start()
        acc[rank + 8 :] += total - jnp.concatenate(wants, axis=0) * jnp.log1p(total)
        return slopes

    def slope_stage(q):
        p = pair_of(q)

        @pl.when(q == 0)
        def _():
            got(tgt.at[pl.ds(0, n - 1)], tgt_r.at[0])

        wants = [tgt[window(p, u)].astype(F32) for u in range(2)]
        want = jnp.concatenate(wants, axis=0)
        got(covr.at[p, pl.ds(0, m - 1)], cov_r.at[p])
        total = covr[p, 0]
        for j in range(1, m):
            total += covr[p, j]
        slp[p, s] = scale * (1.0 - want / (1.0 + total))
        for k in range(1, m):
            slp_copy(p, k).start()
        covt[p] = total
        acc[rank + 8 :] += total - want * jnp.log1p(total)

        @pl.when(q > 0)
        def _():
            out_copy(p, window(p, 0)).start()

        out_copy(p, window(p, 1)).start()

    def grad_rows(p, slopes_of):
        halves = []
        for u in range(2):
            w = window(p, u)
            slopes = slopes_of[u]
            s0 = slopes.astype(BF16)
            left = slopes - s0.astype(F32)
            s1 = left.astype(BF16)
            s2 = (left - s1.astype(F32)).astype(BF16)
            mem = aux[w, rank : rank + genes]
            spread = mm_tn(
                jnp.concatenate([mem, mem, mem], axis=0), jnp.concatenate([s0, s1, s2], axis=0)
            )
            grad = spread * sig[w]
            half = grad.astype(BF16)
            acc[0:rank] += mm(aux[w, 0:rank], half)
            acc[rank : rank + 8] += jnp.sum(grad.reshape(rows // 8, 8, cols), axis=0)
            halves.append(half)
        return halves

    def grad_back(p, halves):
        for u in range(2):
            back = mm_nt(up[...], halves[u])
            high = back.astype(BF16)
            low = (back - high.astype(F32)).astype(BF16)
            side = core if u == 0 else 1 - core
            bkc[:, pl.ds(pl.multiple_of(side * rows, 128), rows)] = jnp.concatenate(
                [high, low], axis=0
            )
        both = mm(bkc[...], hid[pl.ds(2 * p, 2)].reshape(2 * rows, chans))
        both = both[0:rank] + both[rank:]
        for k in range(CHUNKS):
            y, x = (k % 2) * tall, (k // 2) * wide
            dn[k] += both[y : y + tall, x : x + wide]

    def slopes_in(q):
        p = pair_of(q)
        got(slp.at[p, pl.ds(0, m - 1)], slp_r.at[p])
        return [
            jnp.concatenate([slp[p, j][u * owned : (u + 1) * owned] for j in range(m)], axis=0)
            for u in range(2)
        ]

    def grad_stage(q):
        p = pair_of(q)
        grad_back(p, grad_rows(p, slopes_in(q)))

    def step(q, carry):
        head_stage(q)

        @pl.when(q >= 2)
        def _():
            slope_stage(q - 2)

        if last > 4:

            @pl.when(q >= 4)
            def _():
                grad_stage(q - 4)

        return carry

    lax.fori_loop(0, last, step, 0)
    head_last()
    slope_stage(last - 1)
    for q in range(max(0, last - 4), last - 1):
        grad_stage(q)
    grad_back(pair_of(last), grad_rows(pair_of(last), slope_last()))
    grad_stage(last - 1)


    def part_copy(j):
        return send(dn.at[j], dnr.at[d], ds_s.at[0], ds_r.at[0], j, s)

    def if_owner(f):
        if n > CHUNKS:
            pl.when(d < CHUNKS)(f)
        else:
            f()

    def if_other(j, f):
        pl.when(d != j)(f)

    if n == CHUNKS:
        for k in range(1, n):
            part_copy(dp_peer(k)).start()
    else:
        for j in range(CHUNKS):
            if_other(j, lambda: part_copy(j).start())

    ups[s, :, 0:cols] = acc[0:tall]
    bias_sum = jnp.sum(acc[rank : rank + 8], axis=0, keepdims=True)
    loss_sum = scale * jnp.sum(acc[rank + 8 :], axis=0, keepdims=True)
    small = [bias_sum[:, i * 128 : (i + 1) * 128] for i in range(lines)]
    small += [loss_sum[:, i * 128 : (i + 1) * 128] for i in range(lines)]
    if tall > 2 * lines:
        small.append(jnp.zeros((tall - 2 * lines, 128), F32))
    ups[s, :, cols:] = jnp.concatenate(small, axis=0)
    upt[s] = acc[tall:rank]
    for k in range(1, m):
        send(ups.at[s], ups.at[s], us_s.at[0], us_r.at[0], d, seq_peer(k)).start()
    for k in range(1, m):
        send(upt.at[s], upt.at[s], ut_s.at[0], ut_r.at[0], d, seq_peer(k)).start()
    covin[d] = covt[chip]
    got(covin.at[pl.ds(0, n - 1)], co_r.at[0])
    for j in range(n):
        both = covin[j]
        cov_out[0, :, j * cols : (j + 1) * cols] = jnp.where(
            core == j % 2, both[0:owned], both[owned : 2 * owned]
        )

    @pl.when(s < m - 1)
    def _():
        to_next.wait_send()

    @pl.when(s > 0)
    def _():
        to_prev.wait_send()

    sent(binbuf.at[pl.ds(0, m - 1)], bin_s.at[0])
    sent(hid.at[pl.ds(0, n - 1)], hid_s.at[0])
    sent(aux.at[pl.ds(0, n - 1)], aux_s.at[0])
    sent(tgt.at[pl.ds(0, n - 1)], tgt_s.at[0])
    sent(covp.at[pl.ds(0, last), pl.ds(0, m - 1)], cov_s.at[0])
    sent(slp.at[pl.ds(0, last), pl.ds(0, m - 1)], slp_s.at[0])
    sent(tlast, tl_s.at[0])
    sent(covall.at[pl.ds(0, m - 1)], ca_s.at[0])
    sent(covin.at[pl.ds(0, n - 1)], co_s.at[0])

    def gathered_z(k):
        j = seq_peer(k)
        return send(dnz.at[s], dnz.at[s], dz_s.at[0], dz_r.at[0], d, j)

    def spread_part(k):
        return send(dnf.at[d], dnf.at[d], fd_s.at[0], fd_r.at[0], dp_peer(k), s)

    def sum_plane():
        dnr[d] = dn[d]
        got(dnr.at[pl.ds(0, n - 1)], ds_r.at[0])
        total = dnr[0]
        for j in range(1, n):
            total += dnr[j]
        dnz[s] = total
        for k in range(1, m):
            gathered_z(k).start()

    if_owner(sum_plane)

    for held, full, zr, ps, pr in ((ups, fin, us_r, fu_s, fu_r), (upt, fit, ut_r, ft_s, ft_r)):
        got(held.at[pl.ds(0, m - 1)], zr.at[0])
        total = held[0]
        for j in range(1, m):
            total += held[j]
        full[d] = total
        for k in range(1, n):
            send(full.at[d], full.at[d], ps.at[0], pr.at[0], dp_peer(k), s).start()

    def sum_seq():
        got(dnz.at[pl.ds(0, m - 1)], dz_r.at[0])
        total = dnz[0]
        for j in range(1, m):
            total += dnz[j]
        dnf[d] = total
        for k in range(1, n):
            spread_part(k).start()

    if_owner(sum_seq)

    def if_sender(f, g):
        if n > CHUNKS:
            pl.when(d < CHUNKS)(f)
            pl.when(d >= CHUNKS)(g)
        else:
            f()

    sent(ups.at[pl.ds(0, m - 1)], us_s.at[0])
    sent(upt.at[pl.ds(0, m - 1)], ut_s.at[0])
    if_sender(
        lambda: sent(dn.at[pl.ds(0, CHUNKS - 1)], ds_s.at[0]),
        lambda: sent(dn, ds_s.at[0]),
    )
    if_owner(lambda: sent(dnz.at[pl.ds(0, m - 1)], dz_s.at[0]))

    got(fin.at[pl.ds(0, n - 1)], fu_r.at[0])
    loss = jnp.zeros((lines, 128), F32)
    for j in range(n):
        up_out[0:tall, j * cols : (j + 1) * cols] = fin[j, :, 0:cols]
        for i in range(lines):
            x = j * cols + i * 128
            bias_out[:, x : x + 128] = fin[j, i : i + 1, cols:]
        loss += fin[j, lines : 2 * lines, cols:]
    got(fit.at[pl.ds(0, n - 1)], ft_r.at[0])
    for j in range(n):
        up_out[tall:rank, j * cols : (j + 1) * cols] = fit[j]
    loss_out[...] = jnp.sum(jnp.sum(loss, axis=0, keepdims=True), axis=1, keepdims=True)

    if_sender(
        lambda: got(dnf.at[pl.ds(0, CHUNKS - 1)], fd_r.at[0]),
        lambda: got(dnf, fd_r.at[0]),
    )
    for j in range(CHUNKS):
        y, x = (j % 2) * tall, (j // 2) * wide
        down_out[y : y + tall, x : x + wide] = dnf[j]

    sent(fin.at[pl.ds(0, n - 1)], fu_s.at[0])
    sent(fit.at[pl.ds(0, n - 1)], ft_s.at[0])
    if_owner(lambda: sent(dnr.at[pl.ds(0, n - 1)], fd_s.at[0]))


def emit(*refs):
    sems = refs[-1]
    k = (len(refs) - 1) // 2
    copies = [
        pltpu.make_async_copy(refs[i], refs[k + i], sems.at[i]) for i in range(k)
    ]
    for c in copies:
        c.start()
    for c in copies:
        c.wait()


def local(
    n,
    m,
    coarse,
    skip_feats,
    conv_taps,
    norm_gain,
    head_weight,
    adapter_down,
    adapter_up,
    head_bias,
    exon_bins,
    exon_count,
    targets,
):
    rows, chans = skip_feats.shape[1:]
    cols = head_weight.shape[1]
    tracks = adapter_up.shape[1]
    rank = adapter_up.shape[0]
    owned = exon_bins.shape[1]
    genes = owned * m
    nc = n // 2
    wide = chans // (CHUNKS // 2)
    scale = 1.0 / (n * genes)
    vm = pl.BlockSpec(memory_space=pltpu.VMEM)
    hbm = pl.BlockSpec(memory_space=pltpu.HBM)
    dma = pltpu.SemaphoreType.DMA
    cov, loss, down, up, bias = pl.pallas_call(
        functools.partial(kernel, n, m, scale),
        out_shape=(
            pltpu.VMEM((1, owned, tracks), F32),
            pltpu.VMEM((1, 1), F32),
            pltpu.VMEM((rank, chans), F32),
            pltpu.VMEM((rank, tracks), F32),
            pltpu.VMEM((1, tracks), F32),
        ),
        in_specs=[hbm] * 11,
        out_specs=(vm,) * 5,
        scratch_shapes=[
            pltpu.VMEM((1, rows // 2, chans), BF16),
            pltpu.VMEM((1, rows, chans), BF16),
            pltpu.VMEM(conv_taps.shape, F32),
            pltpu.VMEM((chans,), F32),
            pltpu.VMEM((rank, chans), BF16),
            pltpu.VMEM((rank, cols), BF16),
            pltpu.VMEM((1, cols), F32),
            pltpu.VMEM(exon_bins.shape, jnp.int32),
            pltpu.VMEM(exon_count.shape, jnp.int32),
            pltpu.VMEM((chans, cols), BF16),
            pltpu.VMEM((genes, tracks), jnp.int32),
            pltpu.VMEM((n, rows, chans), BF16),
            pltpu.VMEM((n, rank + genes, rows), BF16),
            pltpu.VMEM((2, 1, chans), F32),
            pltpu.VMEM((2, 1, chans), F32),
            pltpu.VMEM((m, 8, 128), jnp.int32),
            pltpu.VMEM((n, owned, cols), jnp.int32),
            pltpu.VMEM((n, owned, cols), jnp.int32),
            pltpu.VMEM((2, genes, cols), jnp.int32),
            pltpu.VMEM((2, genes, cols), jnp.int32),
            pltpu.VMEM((2, genes, cols), F32),
            pltpu.VMEM((m, 2, genes, cols), F32),
            pltpu.VMEM((n, rows, cols), F32),
            pltpu.VMEM((nc, m, 2 * owned, cols), F32),
            pltpu.VMEM((nc, m, 2 * owned, cols), F32),
            pltpu.VMEM((nc, 2 * owned, cols), F32),
            pltpu.VMEM((nc, m, 2 * owned, cols), F32),
            pltpu.VMEM((n, 2 * owned, cols), F32),
            pltpu.VMEM((rank + 16, cols), F32),
            pltpu.VMEM((2 * rank, 2 * rows), BF16),
            pltpu.VMEM((CHUNKS, rank // 2, wide), F32),
            pltpu.VMEM((n, rank // 2, wide), F32),
            pltpu.VMEM((m, rank // 2, wide), F32),
            pltpu.VMEM((CHUNKS, rank // 2, wide), F32),
            pltpu.VMEM((m, rank // 2, cols + 128), F32),
            pltpu.VMEM((m, rank // 2, cols), F32),
            pltpu.VMEM((n, rank // 2, cols + 128), F32),
            pltpu.VMEM((n, rank // 2, cols), F32),
            dma((11,)),
            dma((2,)),
            dma((2,)),
            dma((1,)),
            dma((1,)),
            dma((1,)),
            dma((13 if nc == 4 else n - 1,)),
            dma((1,)),
            dma((3,)),
            dma((1,)),
            dma((1,)),
            dma((1,)),
            dma((1,)),
            dma((1,)),
            dma((1,)),
            dma((1,)),
            dma((nc,)),
            dma((1,)),
            dma((nc,)),
        ]
        + [dma((1,))] * 16,
        compiler_params=pltpu.CompilerParams(
            collective_id=0, has_side_effects=True, vmem_limit_bytes=56 * 2**20
        ),
    )(
        coarse,
        skip_feats,
        conv_taps,
        norm_gain,
        head_weight,
        adapter_down.T,
        adapter_up,
        head_bias.reshape(1, tracks),
        exon_bins,
        exon_count,
        targets,
    )
    held = (cov, loss, down, up, bias)
    cov, loss, down, up, bias = pl.pallas_call(
        emit,
        in_specs=[vm] * 5,
        out_shape=tuple(jax.ShapeDtypeStruct(a.shape, a.dtype) for a in held),
        out_specs=(hbm,) * 5,
        scratch_shapes=[dma((5,))],
    )(*[pltpu.with_memory_space_constraint(h, pltpu.VMEM) for h in held])
    return cov, loss[0, 0], down.T, up, bias.reshape(tracks)


def solution(mesh):
    placed = (
        P("dp", "seq", None),
        P("dp", "seq", None),
        P(),
        P(),
        P(None, "dp"),
        P(),
        P(),
        P(),
        P("dp", "seq", None),
        P("dp", "seq"),
        P("dp", None, None),
    )
    return jax.shard_map(
        functools.partial(local, mesh.shape["dp"], mesh.shape["seq"]),
        mesh=mesh,
        in_specs=placed,
        out_specs=(P("dp", "seq", None), P(), P(), P(), P()),
        check_vma=False,
    )
```

```python
import functools

import jax
import jax.numpy as jnp
from jax import lax
from jax.experimental import pallas as pl
from jax.experimental.pallas import tpu as pltpu
from jax.sharding import PartitionSpec as P

MESH = pl.DeviceIdType.MESH
F32 = jnp.float32
BF16 = jnp.bfloat16
CHUNKS = 8
EDGE = 16


def mm(a, b):
    return jnp.dot(a, b, preferred_element_type=F32)


def mm_nt(a, b):
    return lax.dot_general(a, b, (((1,), (1,)), ((), ())), preferred_element_type=F32)


def mm_tn(a, b):
    return lax.dot_general(a, b, (((0,), (0,)), ((), ())), preferred_element_type=F32)


def kernel(
    n,
    m,
    scale,
    coarse_h,
    skip_h,
    taps_h,
    gain_h,
    weight,
    down_h,
    up_h,
    bias_h,
    bins_h,
    count_h,
    targets,
    cov_out,
    loss_out,
    down_out,
    up_out,
    bias_out,
    coarse,
    skip,
    taps,
    gain,
    down,
    up,
    bias,
    bins,
    count,
    w_vm,
    tfull,
    hid,
    aux,
    halo,
    edge,
    binbuf,
    tsel,
    tgt,
    tlast,
    tin,
    covl,
    covall,
    sig,
    covp,
    covr,
    covt,
    slp,
    covin,
    acc,
    bkc,
    dn,
    dnr,
    dnz,
    dnf,
    ups,
    upt,
    fin,
    fit,
    sem_loc,
    halo_s,
    halo_r,
    bin_s,
    bin_r,
    hid_s,
    hid_r,
    aux_s,
    aux_r,
    tgt_s,
    tgt_r,
    tl_s,
    tl_r,
    ca_s,
    ca_r,
    cov_s,
    cov_r,
    slp_s,
    slp_r,
    co_s,
    co_r,
    us_s,
    us_r,
    fu_s,
    fu_r,
    ut_s,
    ut_r,
    ft_s,
    ft_r,
    ds_s,
    ds_r,
    dz_s,
    dz_r,
    fd_s,
    fd_r,
):
    d = lax.axis_index("dp")
    s = lax.axis_index("seq")
    nc = n // 2
    relay = nc == 4
    chip = d // 2
    core = d % 2
    sib = chip * 2 + (1 - core)
    rows, chans = skip.shape[1], skip.shape[2]
    cols = weight.shape[1]
    owned = bins.shape[1]
    slots = bins.shape[2]
    rank = up.shape[0]
    genes = owned * m
    inner = rows - 2 * EDGE
    mid = inner // 2
    lines = cols // 128
    wide = chans // (CHUNKS // 2)
    tall = rank // 2

    def pair_of(q):
        found, bit = 0, 1
        while bit < nc:
            found = found + bit * (((chip // bit) % 2 + (q // bit) % 2) % 2)
            bit *= 2
        return found

    def send(src, dst, ss, rs, dd, jj):
        return pltpu.make_async_remote_copy(
            src_ref=src,
            dst_ref=dst,
            send_sem=ss,
            recv_sem=rs,
            device_id=(dd, jj),
            device_id_type=MESH,
        )

    def sent(ref, sem):
        send(ref, ref, sem, sem, sib, s).wait_send()

    def got(ref, sem):
        send(ref, ref, sem, sem, sib, s).wait_recv()

    def dp_peer(k):
        return (d + k) % n

    def seq_peer(k):
        return (s + k) % m

    def column(k):
        return pl.ds(pl.multiple_of(k * cols, 128), cols)

    last = nc - 1
    loads = []
    for src, dst in (
        (skip_h, skip),
        (coarse_h, coarse),
        (taps_h, taps),
        (gain_h, gain),
        (bins_h, bins),
        (count_h, count),
        (down_h, down),
        (targets.at[0], tfull),
        (up_h.at[:, column(d)], up),
        (bias_h.at[:, column(d)], bias),
        (weight, w_vm),
    ):
        c = pltpu.make_async_copy(src, dst, sem_loc.at[len(loads)])
        c.start()
        loads.append(c)
    barrier = pltpu.get_barrier_semaphore()
    for k in range(1, m):
        pl.semaphore_signal(barrier, inc=1, device_id=(d, seq_peer(k)), device_id_type=MESH)
    for k in range(1, n):
        pl.semaphore_signal(barrier, inc=1, device_id=(dp_peer(k), s), device_id_type=MESH)

    for c in loads[:2]:
        c.wait()
    rr = lax.broadcasted_iota(jnp.int32, (rows, rows // 2), 0)
    cc = lax.broadcasted_iota(jnp.int32, (rows, rows // 2), 1)
    spread2 = jnp.where(rr // 2 == cc, 1.0, 0.0).astype(BF16)
    merged = (mm(spread2, coarse[0]) + skip[0].astype(F32)).astype(BF16).astype(F32)
    edge[0] = merged[0:1]
    edge[1] = merged[rows - 1 : rows]

    for c in loads[2:6]:
        c.wait()

    def activate(before, at, after):
        mixed = taps[0:1] * before + taps[1:2] * at + taps[2:3] * after
        normed = (
            mixed
            * lax.rsqrt(jnp.mean(mixed * mixed, axis=-1, keepdims=True) + 1e-06)
            * gain[...].reshape(1, chans)
        )
        return jax.nn.gelu(normed).astype(BF16)

    hid[d, 0:inner] = activate(
        pltpu.roll(merged, 1, 0)[EDGE : rows - EDGE],
        merged[EDGE : rows - EDGE],
        pltpu.roll(merged, rows - 1, 0)[EDGE : rows - EDGE],
    )

    cnt = jnp.broadcast_to(count[...].astype(F32), (owned, owned))
    er = lax.broadcasted_iota(jnp.int32, (owned, owned), 0)
    ec = lax.broadcasted_iota(jnp.int32, (owned, owned), 1)
    cnt = jnp.sum(jnp.where(er == ec, cnt, 0.0), axis=1, keepdims=True)
    slot = lax.broadcasted_iota(jnp.int32, (owned, slots), 1).astype(F32)
    binbuf[s] = jnp.full((8, 128), -1, jnp.int32)
    binbuf[s, 0:owned, 0:slots] = jnp.where(slot < cnt, bins[0], -1)

    first, second = pl.ds(0, mid), pl.ds(mid, mid)
    whole, rim = pl.ds(0, inner), pl.ds(inner, 2 * EDGE)
    rims = (pl.ds(inner, EDGE), pl.ds(inner + EDGE, EDGE))

    def block_copy(w, part, sem, to):
        return send(hid.at[w, part], hid.at[w, part], hid_s.at[0], hid_r.at[sem], to, s)

    base = 6 if relay else nc - 1

    def own_copy(k, part, lane):
        if k == 0:
            return block_copy(d, part, base, sib)
        return block_copy(d, part, 3 * (k - 1) + lane if relay else k - 1, 2 * pair_of(k) + core)

    def forward(w, part, q):
        return block_copy(w, part, base + q, sib)

    def arrive(w, part, sem):
        got(hid.at[w, part], hid_r.at[sem])

    def relay_copy(k, lane):
        w = 2 * pair_of(k) + core
        part = ((first, second)[k - 1], rims[k - 1])[lane]
        return block_copy(w, part, 12 if lane else 9 + k, 2 * pair_of(3 - k) + core)

    pl.semaphore_wait(barrier, n + m - 2)

    to_next = send(edge.at[1], halo.at[0], halo_s.at[0], halo_r.at[0], d, (s + 1) % m)
    to_prev = send(edge.at[0], halo.at[1], halo_s.at[1], halo_r.at[1], d, (s + m - 1) % m)

    @pl.when(s < m - 1)
    def _():
        to_next.start()

    @pl.when(s > 0)
    def _():
        to_prev.start()

    if relay:
        own_copy(1, first, 0).start()
        own_copy(2, second, 1).start()
        own_copy(1, second, 1).start()
        own_copy(2, first, 0).start()
    else:
        for k in range(1, nc):
            own_copy(k, whole, 0).start()
    own_copy(0, whole, 0).start()

    for k in range(1, m):
        send(binbuf.at[s], binbuf.at[s], bin_s.at[0], bin_r.at[0], d, seq_peer(k)).start()

    @pl.when(s == 0)
    def _():
        halo[0] = jnp.zeros((1, chans), F32)

    @pl.when(s == m - 1)
    def _():
        halo[1] = jnp.zeros((1, chans), F32)

    for c in loads[6:8]:
        c.wait()
    def owned_rows(x):
        found = x[0:owned]
        for j in range(1, m):
            found = jnp.where(s == j, x[j * owned : (j + 1) * owned], found)
        return found

    want = owned_rows(tfull[...])
    for j in range(n):
        tsel[j] = want[:, j * cols : (j + 1) * cols]
    tgt[d] = tsel[d]
    for c in (0, 1):
        tlast[c] = tfull[:, column(2 * pair_of(last) + c)]
    acc[...] = jnp.zeros(acc.shape, F32)
    dn[...] = jnp.zeros(dn.shape, F32)

    @pl.when(s > 0)
    def _():
        to_next.wait_recv()

    @pl.when(s < m - 1)
    def _():
        to_prev.wait_recv()

    reach = EDGE + 8
    row = lax.broadcasted_iota(jnp.int32, (reach, chans), 0)
    top, low = merged[0:reach], merged[rows - reach :]
    hid[d, inner + EDGE :] = activate(
        jnp.where(row == 0, halo[0], pltpu.roll(top, 1, 0))[0:EDGE],
        top[0:EDGE],
        pltpu.roll(top, reach - 1, 0)[0:EDGE],
    )
    hid[d, inner : inner + EDGE] = activate(
        pltpu.roll(low, 1, 0)[8:],
        low[8:],
        jnp.where(row == reach - 1, halo[1], pltpu.roll(low, reach - 1, 0))[8:],
    )
    for k in range(1, 3 if relay else nc):
        own_copy(k, rim, 2).start()
    own_copy(0, rim, 2).start()

    aux[d, 0:rank] = mm_nt(down[...], hid[d]).astype(BF16)

    got(binbuf.at[pl.ds(0, m - 1)], bin_r.at[0])
    listed = jnp.concatenate([binbuf[j][0:owned] for j in range(m)], axis=0)
    here = s * rows + (lax.broadcasted_iota(jnp.int32, (genes, rows), 1) + EDGE) % rows
    member = jnp.zeros((genes, rows), F32)
    for j in range(slots):
        member += jnp.where(listed[:, j : j + 1] == here, 1.0, 0.0)
    aux[d, rank : rank + genes] = member.astype(BF16)

    def aux_copy(w, to, sem):
        return send(aux.at[w], aux.at[w], aux_s.at[0], aux_r.at[sem], to, s)

    def tgt_copy(src, w, to, sem):
        return send(src, tgt.at[w], tgt_s.at[0], tgt_r.at[sem], to, s)

    aux_copy(d, sib, 1).start()
    for k in range(1, nc):
        aux_copy(d, 2 * pair_of(k) + core, 0).start()
    for k in range(1, n):
        j = dp_peer(k)
        tgt_copy(tsel.at[j], d, j, 0).start()

    for c in loads[8:]:
        c.wait()

    def window(p, u):
        return 2 * p + (core if u == 0 else 1 - core)

    def cov_copy(p, j):
        return send(covp.at[p, j], covr.at[p, s], cov_s.at[0], cov_r.at[p], d, j)

    def slp_copy(p, k):
        return send(slp.at[p, s], slp.at[p, s], slp_s.at[0], slp_r.at[p], d, seq_peer(k))

    def out_copy(p, w):
        return send(covt.at[p], covin.at[d], co_s.at[0], co_r.at[0], w, s)

    def tlast_copy(c):
        return send(tlast.at[c], tin.at[core], tl_s.at[0], tl_r.at[0], 2 * pair_of(last) + c, s)

    def all_copy(u, k):
        return send(covl.at[u], covall.at[s, u], ca_s.at[0], ca_r.at[0], d, seq_peer(k))

    def head(w):
        out = mm(hid[w], w_vm[...])
        out += mm_tn(aux[w, 0:rank], up[...])
        out += bias[...]
        e = jnp.exp(-jnp.abs(out))
        r = 1.0 / (1.0 + e)
        sig[w] = jnp.where(out >= 0, r, e * r)
        predicted = jnp.maximum(out, 0.0) + jnp.log1p(e)
        high = predicted.astype(BF16)
        low = (predicted - high.astype(F32)).astype(BF16)
        mem = aux[w, rank : rank + genes]
        return mm(mem, high) + mm(mem, low)

    def head_stage(q):
        p = pair_of(q)
        parts = []
        for u in range(2):
            w = window(p, u)

            if u == 0:

                if relay:

                    @pl.when(q == 1)
                    def _():
                        near = [2 * pair_of(k) + core for k in (1, 2)]
                        arrive(near[0], second, 1)
                        forward(near[0], whole, 1).start()
                        arrive(near[1], first, 3)
                        forward(near[1], whole, 2).start()
                        for k in (1, 2):
                            arrive(near[k - 1], rim, 3 * k - 1)
                            relay_copy(k, 1).start()
                            forward(near[k - 1], rim, k).start()

                else:

                    @pl.when(q > 0)
                    def _():
                        got(hid.at[w], hid_r.at[q - 1])
                        send(hid.at[w], hid.at[w], hid_s.at[0], hid_r.at[base + q], sib, s).start()

                @pl.when(q == 1)
                def _():
                    got(aux.at[pl.ds(0, nc - 1)], aux_r.at[0])
                    for k in range(1, nc):
                        aux_copy(2 * pair_of(k) + core, sib, 2).start()
                    for c in (0, 1):
                        tlast_copy(c).start()

            else:
                if relay:

                    @pl.when(q == 0)
                    def _():
                        arrive(2 * pair_of(1) + core, first, 0)
                        relay_copy(1, 0).start()
                        arrive(2 * pair_of(2) + core, second, 4)
                        relay_copy(2, 0).start()

                got(hid.at[w], hid_r.at[base + q])

                @pl.when(q == 0)
                def _():
                    got(aux.at[0], aux_r.at[1])

                @pl.when(q == 1)
                def _():
                    got(aux.at[pl.ds(0, nc - 1)], aux_r.at[2])

            parts.append(head(w))
        for j in range(m):
            covp[p, j] = jnp.concatenate(
                [part[j * owned : (j + 1) * owned] for part in parts], axis=0
            )
        covr[p, s] = covp[p, s]
        for k in range(1, m):
            cov_copy(p, seq_peer(k)).start()

    def head_last():
        p = pair_of(last)
        for u in range(2):
            w = window(p, u)
            if u == 0:
                if relay:
                    arrive(w, first, 10)
                    forward(w, first, 3).start()
                    arrive(w, second, 11)
                    forward(w, second, 3).start()
                    arrive(w, rim, 12)
                    forward(w, rim, 3).start()
                else:
                    got(hid.at[w], hid_r.at[last - 1])
                    send(hid.at[w], hid.at[w], hid_s.at[0], hid_r.at[base + last], sib, s).start()
            else:
                if last >= 2:
                    slope_stage(last - 2)
                got(hid.at[w], hid_r.at[base + last])
            part = head(w)
            covl[u] = part
            covall[s, u] = part
            for k in range(1, m):
                all_copy(u, k).start()

    def slope_last():
        p = pair_of(last)
        got(tin, tl_r.at[0])
        got(covall.at[pl.ds(0, m - 1)], ca_r.at[0])
        slopes, totals, wants = [], [], []
        for u in range(2):
            total = covall[0, u]
            for j in range(1, m):
                total += covall[j, u]
            want = tin[core if u == 0 else 1 - core].astype(F32)
            slopes.append(scale * (1.0 - want / (1.0 + total)))
            totals.append(owned_rows(total))
            wants.append(owned_rows(want))
        total = jnp.concatenate(totals, axis=0)
        covt[p] = total
        for u in range(2):
            out_copy(p, window(p, u)).start()
        acc[rank + 8 :] += total - jnp.concatenate(wants, axis=0) * jnp.log1p(total)
        return slopes

    def slope_stage(q):
        p = pair_of(q)

        @pl.when(q == 0)
        def _():
            got(tgt.at[pl.ds(0, n - 1)], tgt_r.at[0])

        wants = [tgt[window(p, u)].astype(F32) for u in range(2)]
        want = jnp.concatenate(wants, axis=0)
        got(covr.at[p, pl.ds(0, m - 1)], cov_r.at[p])
        total = covr[p, 0]
        for j in range(1, m):
            total += covr[p, j]
        slp[p, s] = scale * (1.0 - want / (1.0 + total))
        for k in range(1, m):
            slp_copy(p, k).start()
        covt[p] = total
        acc[rank + 8 :] += total - want * jnp.log1p(total)

        @pl.when(q > 0)
        def _():
            out_copy(p, window(p, 0)).start()

        out_copy(p, window(p, 1)).start()

    def grad_rows(p, slopes_of):
        halves = []
        for u in range(2):
            w = window(p, u)
            slopes = slopes_of[u]
            s0 = slopes.astype(BF16)
            left = slopes - s0.astype(F32)
            s1 = left.astype(BF16)
            s2 = (left - s1.astype(F32)).astype(BF16)
            mem = aux[w, rank : rank + genes]
            spread = mm_tn(
                jnp.concatenate([mem, mem, mem], axis=0), jnp.concatenate([s0, s1, s2], axis=0)
            )
            grad = spread * sig[w]
            half = grad.astype(BF16)
            acc[0:rank] += mm(aux[w, 0:rank], half)
            acc[rank : rank + 8] += jnp.sum(grad.reshape(rows // 8, 8, cols), axis=0)
            halves.append(half)
        return halves

    def grad_back(p, halves):
        for u in range(2):
            back = mm_nt(up[...], halves[u])
            high = back.astype(BF16)
            low = (back - high.astype(F32)).astype(BF16)
            side = core if u == 0 else 1 - core
            bkc[:, pl.ds(pl.multiple_of(side * rows, 128), rows)] = jnp.concatenate(
                [high, low], axis=0
            )
        both = mm(bkc[...], hid[pl.ds(2 * p, 2)].reshape(2 * rows, chans))
        both = both[0:rank] + both[rank:]
        for k in range(CHUNKS):
            y, x = (k % 2) * tall, (k // 2) * wide
            dn[k] += both[y : y + tall, x : x + wide]

    def slopes_in(q):
        p = pair_of(q)
        got(slp.at[p, pl.ds(0, m - 1)], slp_r.at[p])
        return [
            jnp.concatenate([slp[p, j][u * owned : (u + 1) * owned] for j in range(m)], axis=0)
            for u in range(2)
        ]

    def grad_stage(q):
        p = pair_of(q)
        grad_back(p, grad_rows(p, slopes_in(q)))

    def step(q, carry):
        head_stage(q)

        @pl.when(q >= 2)
        def _():
            slope_stage(q - 2)

        if last > 4:

            @pl.when(q >= 4)
            def _():
                grad_stage(q - 4)

        return carry

    lax.fori_loop(0, last, step, 0)
    head_last()
    slope_stage(last - 1)
    for q in range(max(0, last - 4), last - 1):
        grad_stage(q)
    grad_back(pair_of(last), grad_rows(pair_of(last), slope_last()))
    grad_stage(last - 1)


    others = [2 * pair_of(k) + c for k in range(nc - 1, 0, -1) for c in (0, 1)] + [sib]

    def part_copy(j):
        return send(dn.at[j], dnr.at[d], ds_s.at[0], ds_r.at[0], j, s)

    def if_owner(f):
        if n > CHUNKS:
            pl.when(d < CHUNKS)(f)
        else:
            f()

    def if_other(j, f):
        pl.when(d != j)(f)

    if n == CHUNKS:
        for j in others:
            part_copy(j).start()
    else:
        for j in range(CHUNKS):
            if_other(j, lambda: part_copy(j).start())

    ups[s, :, 0:cols] = acc[0:tall]
    bias_sum = jnp.sum(acc[rank : rank + 8], axis=0, keepdims=True)
    loss_sum = scale * jnp.sum(acc[rank + 8 :], axis=0, keepdims=True)
    small = [bias_sum[:, i * 128 : (i + 1) * 128] for i in range(lines)]
    small += [loss_sum[:, i * 128 : (i + 1) * 128] for i in range(lines)]
    if tall > 2 * lines:
        small.append(jnp.zeros((tall - 2 * lines, 128), F32))
    ups[s, :, cols:] = jnp.concatenate(small, axis=0)
    upt[s] = acc[tall:rank]
    for k in range(1, m):
        send(ups.at[s], ups.at[s], us_s.at[0], us_r.at[0], d, seq_peer(k)).start()
    for k in range(1, m):
        send(upt.at[s], upt.at[s], ut_s.at[0], ut_r.at[0], d, seq_peer(k)).start()
    covin[d] = covt[chip]
    got(covin.at[pl.ds(0, n - 1)], co_r.at[0])
    for j in range(n):
        both = covin[j]
        cov_out[0, :, j * cols : (j + 1) * cols] = jnp.where(
            core == j % 2, both[0:owned], both[owned : 2 * owned]
        )

    @pl.when(s < m - 1)
    def _():
        to_next.wait_send()

    @pl.when(s > 0)
    def _():
        to_prev.wait_send()

    sent(binbuf.at[pl.ds(0, m - 1)], bin_s.at[0])
    sent(hid.at[pl.ds(0, n - 1)], hid_s.at[0])
    sent(aux.at[pl.ds(0, n - 1)], aux_s.at[0])
    sent(tgt.at[pl.ds(0, n - 1)], tgt_s.at[0])
    sent(covp.at[pl.ds(0, last), pl.ds(0, m - 1)], cov_s.at[0])
    sent(slp.at[pl.ds(0, last), pl.ds(0, m - 1)], slp_s.at[0])
    sent(tlast, tl_s.at[0])
    sent(covall.at[pl.ds(0, m - 1)], ca_s.at[0])
    sent(covin.at[pl.ds(0, n - 1)], co_s.at[0])

    def gathered_z(k):
        j = seq_peer(k)
        return send(dnz.at[s], dnz.at[s], dz_s.at[0], dz_r.at[0], d, j)

    def spread_part(j):
        return send(dnf.at[d], dnf.at[d], fd_s.at[0], fd_r.at[0], j, s)

    def sum_plane():
        dnr[d] = dn[d]
        got(dnr.at[pl.ds(0, n - 1)], ds_r.at[0])
        total = dnr[0]
        for j in range(1, n):
            total += dnr[j]
        dnz[s] = total
        for k in range(1, m):
            gathered_z(k).start()

    if_owner(sum_plane)

    for held, full, zr, ps, pr in ((ups, fin, us_r, fu_s, fu_r), (upt, fit, ut_r, ft_s, ft_r)):
        got(held.at[pl.ds(0, m - 1)], zr.at[0])
        total = held[0]
        for j in range(1, m):
            total += held[j]
        full[d] = total
        for j in others:
            send(full.at[d], full.at[d], ps.at[0], pr.at[0], j, s).start()

    def sum_seq():
        got(dnz.at[pl.ds(0, m - 1)], dz_r.at[0])
        total = dnz[0]
        for j in range(1, m):
            total += dnz[j]
        dnf[d] = total
        for j in others:
            spread_part(j).start()

    if_owner(sum_seq)

    def if_sender(f, g):
        if n > CHUNKS:
            pl.when(d < CHUNKS)(f)
            pl.when(d >= CHUNKS)(g)
        else:
            f()

    sent(ups.at[pl.ds(0, m - 1)], us_s.at[0])
    sent(upt.at[pl.ds(0, m - 1)], ut_s.at[0])
    if_sender(
        lambda: sent(dn.at[pl.ds(0, CHUNKS - 1)], ds_s.at[0]),
        lambda: sent(dn, ds_s.at[0]),
    )
    if_owner(lambda: sent(dnz.at[pl.ds(0, m - 1)], dz_s.at[0]))

    got(fin.at[pl.ds(0, n - 1)], fu_r.at[0])
    loss = jnp.zeros((lines, 128), F32)
    for j in range(n):
        up_out[0:tall, j * cols : (j + 1) * cols] = fin[j, :, 0:cols]
        for i in range(lines):
            x = j * cols + i * 128
            bias_out[:, x : x + 128] = fin[j, i : i + 1, cols:]
        loss += fin[j, lines : 2 * lines, cols:]
    got(fit.at[pl.ds(0, n - 1)], ft_r.at[0])
    for j in range(n):
        up_out[tall:rank, j * cols : (j + 1) * cols] = fit[j]
    loss_out[...] = jnp.sum(jnp.sum(loss, axis=0, keepdims=True), axis=1, keepdims=True)

    if_sender(
        lambda: got(dnf.at[pl.ds(0, CHUNKS - 1)], fd_r.at[0]),
        lambda: got(dnf, fd_r.at[0]),
    )
    for j in range(CHUNKS):
        y, x = (j % 2) * tall, (j // 2) * wide
        down_out[y : y + tall, x : x + wide] = dnf[j]

    sent(fin.at[pl.ds(0, n - 1)], fu_s.at[0])
    sent(fit.at[pl.ds(0, n - 1)], ft_s.at[0])
    if_owner(lambda: sent(dnr.at[pl.ds(0, n - 1)], fd_s.at[0]))


def emit(*refs):
    sems = refs[-1]
    k = (len(refs) - 1) // 2
    copies = [
        pltpu.make_async_copy(refs[i], refs[k + i], sems.at[i]) for i in range(k)
    ]
    for c in copies:
        c.start()
    for c in copies:
        c.wait()


def local(
    n,
    m,
    coarse,
    skip_feats,
    conv_taps,
    norm_gain,
    head_weight,
    adapter_down,
    adapter_up,
    head_bias,
    exon_bins,
    exon_count,
    targets,
):
    rows, chans = skip_feats.shape[1:]
    cols = head_weight.shape[1]
    tracks = adapter_up.shape[1]
    rank = adapter_up.shape[0]
    owned = exon_bins.shape[1]
    genes = owned * m
    nc = n // 2
    wide = chans // (CHUNKS // 2)
    scale = 1.0 / (n * genes)
    vm = pl.BlockSpec(memory_space=pltpu.VMEM)
    hbm = pl.BlockSpec(memory_space=pltpu.HBM)
    dma = pltpu.SemaphoreType.DMA
    cov, loss, down, up, bias = pl.pallas_call(
        functools.partial(kernel, n, m, scale),
        out_shape=(
            pltpu.VMEM((1, owned, tracks), F32),
            pltpu.VMEM((1, 1), F32),
            pltpu.VMEM((rank, chans), F32),
            pltpu.VMEM((rank, tracks), F32),
            pltpu.VMEM((1, tracks), F32),
        ),
        in_specs=[hbm] * 11,
        out_specs=(vm,) * 5,
        scratch_shapes=[
            pltpu.VMEM((1, rows // 2, chans), BF16),
            pltpu.VMEM((1, rows, chans), BF16),
            pltpu.VMEM(conv_taps.shape, F32),
            pltpu.VMEM((chans,), F32),
            pltpu.VMEM((rank, chans), BF16),
            pltpu.VMEM((rank, cols), BF16),
            pltpu.VMEM((1, cols), F32),
            pltpu.VMEM(exon_bins.shape, jnp.int32),
            pltpu.VMEM(exon_count.shape, jnp.int32),
            pltpu.VMEM((chans, cols), BF16),
            pltpu.VMEM((genes, tracks), jnp.int32),
            pltpu.VMEM((n, rows, chans), BF16),
            pltpu.VMEM((n, rank + genes, rows), BF16),
            pltpu.VMEM((2, 1, chans), F32),
            pltpu.VMEM((2, 1, chans), F32),
            pltpu.VMEM((m, 8, 128), jnp.int32),
            pltpu.VMEM((n, owned, cols), jnp.int32),
            pltpu.VMEM((n, owned, cols), jnp.int32),
            pltpu.VMEM((2, genes, cols), jnp.int32),
            pltpu.VMEM((2, genes, cols), jnp.int32),
            pltpu.VMEM((2, genes, cols), F32),
            pltpu.VMEM((m, 2, genes, cols), F32),
            pltpu.VMEM((n, rows, cols), F32),
            pltpu.VMEM((nc, m, 2 * owned, cols), F32),
            pltpu.VMEM((nc, m, 2 * owned, cols), F32),
            pltpu.VMEM((nc, 2 * owned, cols), F32),
            pltpu.VMEM((nc, m, 2 * owned, cols), F32),
            pltpu.VMEM((n, 2 * owned, cols), F32),
            pltpu.VMEM((rank + 16, cols), F32),
            pltpu.VMEM((2 * rank, 2 * rows), BF16),
            pltpu.VMEM((CHUNKS, rank // 2, wide), F32),
            pltpu.VMEM((n, rank // 2, wide), F32),
            pltpu.VMEM((m, rank // 2, wide), F32),
            pltpu.VMEM((CHUNKS, rank // 2, wide), F32),
            pltpu.VMEM((m, rank // 2, cols + 128), F32),
            pltpu.VMEM((m, rank // 2, cols), F32),
            pltpu.VMEM((n, rank // 2, cols + 128), F32),
            pltpu.VMEM((n, rank // 2, cols), F32),
            dma((11,)),
            dma((2,)),
            dma((2,)),
            dma((1,)),
            dma((1,)),
            dma((1,)),
            dma((13 if nc == 4 else n - 1,)),
            dma((1,)),
            dma((3,)),
            dma((1,)),
            dma((1,)),
            dma((1,)),
            dma((1,)),
            dma((1,)),
            dma((1,)),
            dma((1,)),
            dma((nc,)),
            dma((1,)),
            dma((nc,)),
        ]
        + [dma((1,))] * 16,
        compiler_params=pltpu.CompilerParams(
            collective_id=0, has_side_effects=True, vmem_limit_bytes=56 * 2**20
        ),
    )(
        coarse,
        skip_feats,
        conv_taps,
        norm_gain,
        head_weight,
        adapter_down.T,
        adapter_up,
        head_bias.reshape(1, tracks),
        exon_bins,
        exon_count,
        targets,
    )
    held = (cov, loss, down, up, bias)
    cov, loss, down, up, bias = pl.pallas_call(
        emit,
        in_specs=[vm] * 5,
        out_shape=tuple(jax.ShapeDtypeStruct(a.shape, a.dtype) for a in held),
        out_specs=(hbm,) * 5,
        scratch_shapes=[dma((5,))],
    )(*[pltpu.with_memory_space_constraint(h, pltpu.VMEM) for h in held])
    return cov, loss[0, 0], down.T, up, bias.reshape(tracks)


def solution(mesh):
    placed = (
        P("dp", "seq", None),
        P("dp", "seq", None),
        P(),
        P(),
        P(None, "dp"),
        P(),
        P(),
        P(),
        P("dp", "seq", None),
        P("dp", "seq"),
        P("dp", None, None),
    )
    return jax.shard_map(
        functools.partial(local, mesh.shape["dp"], mesh.shape["seq"]),
        mesh=mesh,
        in_specs=placed,
        out_specs=(P("dp", "seq", None), P(), P(), P(), P()),
        check_vma=False,
    )
```
